32 devices in a mesh: seq: 4 (over x, core), chan: 8 (over z, y).
Axes of the slice: x: 2, y: 2, z: 4, core: 2. Of those that a mesh axis runs over, the one named last changes fastest.
Arguments:
- features: bfloat16 [3, 4096, 512], P(None, 'chan', 'seq'), may hold values from -6 to 6
- cotangent: bfloat16 [4096, 512], P('chan', 'seq'), may hold values from -6 to 6
- long_filter: bfloat16 [4096, 512], P('chan', 'seq'), may hold values from -0.25 to 0.25
- short_filters: float32 [3, 4096, 3], P(None, 'chan'), may hold values from -3.5 to 3.5
- skip_gain: float32 [4096], P('chan'), may hold values from -4 to 4
Outputs:
- gated_out: bfloat16 [4096, 512], P('chan', 'seq')
- feature_grad: bfloat16 [3, 4096, 512], P(None, 'chan', 'seq')
- long_grad: bfloat16 [4096, 512], P('chan', 'seq')
- short_grad: float32 [3, 4096, 3], P(None, 'chan')
- skip_grad: float32 [4096], P('chan')
The draws below stay inside these ranges and needn't reach their ends.
All inputs are finite; a program needn't handle non-finite values.
Results may differ from the reference program's by a relative error of at most 0.015.
Values may be sent and summed in bfloat16 or wider, within the bound.
A program may use at most 64 MiB of HBM per device.

```python
import math
import jax
import jax.numpy as jnp
from jax import lax

D = 4096
TAPS = 3
LEN = 512


def block_levels(stream_key, extent, pieces, least, largest):
    factor_of = 1.0
    for position, parts in pieces:
        heights = jax.random.uniform(jax.random.fold_in(jax.random.fold_in(stream_key, 6), position), (parts,), jnp.float32, least / len(pieces), largest / len(pieces))
        factor_of = factor_of * jnp.repeat(jnp.exp(heights), extent[position] // parts).reshape((-1,) + (1,) * (len(extent) - 1 - position))
    return factor_of


def gaussian(stream_key, extent, spread, bound, pieces=(), kind=jnp.bfloat16):
    drawn = spread * jax.random.normal(stream_key, extent, jnp.float32)
    if pieces:
        drawn = drawn * block_levels(stream_key, extent, pieces, -0.22, 0.18)
    return jnp.clip(drawn, -bound, bound).astype(kind)


def setup_inputs(seed: int = 0) -> dict:
    keys = jax.random.split(jax.random.key(seed), 6)
    features = gaussian(keys[0], (3, D, LEN), 1.0, 6.0, ((1, 8), (2, 4)))
    cotangent = gaussian(keys[1], (D, LEN), 1.0, 6.0, ((0, 8), (1, 4)))
    long_filter = gaussian(keys[2], (D, LEN), LEN ** -0.5, 0.25, ((0, 8), (1, 4)))
    short_filters = gaussian(keys[3], (3, D, TAPS), TAPS ** -0.5, 3.5, ((1, 8),), jnp.float32)
    skip_gain = gaussian(keys[4], (D,), 1.0, 4.0, ((0, 8),), jnp.float32)
    return dict(features=features, cotangent=cotangent, long_filter=long_filter, short_filters=short_filters, skip_gain=skip_gain)


def delayed(values, offset):
    if offset == 0:
        return values
    padding = jnp.zeros(values.shape[:-1] + (offset,), values.dtype)
    return jnp.concatenate([padding, values[..., :-offset]], axis=-1)


def advanced(values, offset):
    if offset == 0:
        return values
    padding = jnp.zeros(values.shape[:-1] + (offset,), values.dtype)
    return jnp.concatenate([values[..., offset:], padding], axis=-1)


def long_terms(block):
    mixed_block, gated_block, kernel_block = block
    length = mixed_block.shape[-1]
    mixed_freq = jnp.fft.rfft(mixed_block, n=2 * length, axis=-1)
    gated_freq = jnp.fft.rfft(gated_block, n=2 * length, axis=-1)
    kernel_freq = jnp.fft.rfft(kernel_block, n=2 * length, axis=-1)
    conv_part = jnp.fft.irfft(mixed_freq * kernel_freq, n=2 * length, axis=-1)[:, :length]
    corr_part = jnp.fft.irfft(gated_freq * jnp.conj(kernel_freq), n=2 * length, axis=-1)[:, :length]
    cross_part = jnp.fft.irfft(gated_freq * jnp.conj(mixed_freq), n=2 * length, axis=-1)[:, :length]
    return conv_part.astype(jnp.float32), corr_part.astype(jnp.float32), cross_part.astype(jnp.float32)


def reference(features, cotangent, long_filter, short_filters, skip_gain):
    wide = features.astype(jnp.float32)
    primed = short_filters[:, :, 0:1] * wide
    for offset in range(1, TAPS):
        primed = primed + short_filters[:, :, offset:offset + 1] * delayed(wide, offset)
    mixed_term = (primed[1] * primed[2]).astype(jnp.bfloat16)
    cot_wide = cotangent.astype(jnp.float32)
    gated_grad = (cot_wide * primed[0]).astype(jnp.bfloat16)
    mixed_wide = mixed_term.astype(jnp.float32)
    gated_wide = gated_grad.astype(jnp.float32)
    block_rows = math.gcd(D, 256)
    block_count = D // block_rows
    blocks = (mixed_wide.reshape(block_count, block_rows, LEN),
              gated_wide.reshape(block_count, block_rows, LEN),
              long_filter.astype(jnp.float32).reshape(block_count, block_rows, LEN))
    conv_part, corr_part, cross_part = lax.map(long_terms, blocks)
    conv_part = conv_part.reshape(D, LEN)
    corr_part = corr_part.reshape(D, LEN)
    cross_part = cross_part.reshape(D, LEN)
    gain_column = skip_gain[:, None]
    long_out = (conv_part + gain_column * mixed_wide).astype(jnp.bfloat16)
    mixed_grad = (corr_part + gain_column * gated_wide).astype(jnp.bfloat16)
    long_wide = long_out.astype(jnp.float32)
    gated_out = (primed[0] * long_wide).astype(jnp.bfloat16)
    mixed_back = mixed_grad.astype(jnp.float32)
    primed_grad = jnp.stack([cot_wide * long_wide, mixed_back * primed[2], mixed_back * primed[1]])
    feature_grad = short_filters[:, :, 0:1] * primed_grad
    for offset in range(1, TAPS):
        feature_grad = feature_grad + short_filters[:, :, offset:offset + 1] * advanced(primed_grad, offset)
    short_grad = jnp.stack([jnp.sum(primed_grad * delayed(wide, offset), axis=-1) for offset in range(TAPS)], axis=-1)
    skip_grad = jnp.sum(gated_wide * mixed_wide, axis=-1)
    return gated_out, feature_grad.astype(jnp.bfloat16), cross_part.astype(jnp.bfloat16), short_grad, skip_grad
```

```python
import functools
import math

import jax
import jax.numpy as jnp
import numpy as np
from jax import lax
from jax.experimental import pallas as pl
from jax.experimental.pallas import tpu as pltpu
from jax.sharding import PartitionSpec as P

inner_length = 128
radix_width = 8
chunk_count = 1


def phase_tables(row_count, col_count, length, direction):
    phase_index = (
        lax.iota(jnp.int32, row_count)[:, None] * lax.iota(jnp.int32, col_count)[None, :] % length
    )
    angles = direction * 2.0 * math.pi / length * phase_index.astype(jnp.float32)
    return (jnp.cos(angles), jnp.sin(angles))


def last_axis(operand, matrix):
    return jnp.einsum("...n,nk->...k", operand, matrix, precision=lax.Precision.HIGH)


def first_axis(operand, matrix):
    return jnp.einsum("...ab,ak->...kb", operand, matrix, precision=lax.Precision.HIGH)


def transform(real_part, imag_part, direction):
    length = real_part.shape[-1]
    if length <= inner_length or length % radix_width != 0:
        cos_table, sin_table = phase_tables(length, length, length, direction)
        return (
            last_axis(real_part, cos_table) - last_axis(imag_part, sin_table),
            last_axis(real_part, sin_table) + last_axis(imag_part, cos_table),
        )
    rest_length = length // radix_width
    grid_shape = real_part.shape[:-1] + (radix_width, rest_length)
    real_grid = real_part.reshape(grid_shape)
    imag_grid = imag_part.reshape(grid_shape)
    cos_table, sin_table = phase_tables(radix_width, radix_width, radix_width, direction)
    section_real = first_axis(real_grid, cos_table) - first_axis(imag_grid, sin_table)
    section_imag = first_axis(real_grid, sin_table) + first_axis(imag_grid, cos_table)
    twist_cos, twist_sin = phase_tables(radix_width, rest_length, length, direction)
    turned_real = section_real * twist_cos - section_imag * twist_sin
    turned_imag = section_real * twist_sin + section_imag * twist_cos
    inner_real, inner_imag = transform(turned_real, turned_imag, direction)
    return (
        jnp.swapaxes(inner_real, -1, -2).reshape(real_part.shape),
        jnp.swapaxes(inner_imag, -1, -2).reshape(real_part.shape),
    )


def spectral(mixed_term, gated_grad, kernel, local_gain):
    length = mixed_term.shape[-1]
    mixed_wide = mixed_term.astype(jnp.float32)
    gated_wide = gated_grad.astype(jnp.float32)
    kernel_wide = kernel.astype(jnp.float32)
    extend = ((0, 0), (0, length))
    real_in = jnp.stack([jnp.pad(mixed_wide, extend), jnp.pad(kernel_wide, extend)])
    imag_in = jnp.stack(
        [jnp.pad(gated_wide, extend), jnp.zeros((kernel_wide.shape[0], 2 * length), jnp.float32)]
    )
    freq_real, freq_imag = transform(real_in, imag_in, -1.0)
    packed_real = freq_real[0]
    packed_imag = freq_imag[0]
    mirror_real = jnp.roll(jnp.flip(packed_real, -1), 1, -1)
    mirror_imag = jnp.roll(jnp.flip(packed_imag, -1), 1, -1)
    mix_real = 0.5 * (packed_real + mirror_real)
    mix_imag = 0.5 * (packed_imag - mirror_imag)
    grad_real = 0.5 * (packed_imag + mirror_imag)
    grad_imag = 0.5 * (mirror_real - packed_real)
    kern_real = freq_real[1]
    kern_imag = freq_imag[1]
    conv_real = mix_real * kern_real - mix_imag * kern_imag
    conv_imag = mix_real * kern_imag + mix_imag * kern_real
    corr_real = grad_real * kern_real + grad_imag * kern_imag
    corr_imag = grad_imag * kern_real - grad_real * kern_imag
    cross_real = grad_real * mix_real + grad_imag * mix_imag
    cross_imag = grad_imag * mix_real - grad_real * mix_imag
    back_real = jnp.stack([conv_real - corr_imag, cross_real])
    back_imag = jnp.stack([conv_imag + corr_real, cross_imag])
    time_real, time_imag = transform(back_real, back_imag, 1.0)
    inverse_scale = 1.0 / (2 * length)
    conv_part = time_real[0, :, :length] * inverse_scale
    corr_part = time_imag[0, :, :length] * inverse_scale
    cross_part = time_real[1, :, :length] * inverse_scale
    gain_column = local_gain[:, None]
    long_out = (conv_part + gain_column * mixed_wide).astype(jnp.bfloat16)
    mixed_grad = (corr_part + gain_column * gated_wide).astype(jnp.bfloat16)
    return (long_out, mixed_grad, cross_part.astype(jnp.bfloat16))


def featurize(history, weights, margin, span_count):
    running = weights[:, :, 0:1] * history[:, :, margin : margin + span_count]
    for offset in range(1, margin + 1):
        running = (
            running
            + weights[:, :, offset : offset + 1]
            * history[:, :, margin - offset : margin - offset + span_count]
        )
    return running


def unfeaturize(padded_grad, weights, span_count):
    running = weights[:, :, 0:1] * padded_grad[:, :, 0:span_count]
    for offset in range(1, weights.shape[2]):
        running = (
            running
            + weights[:, :, offset : offset + 1] * padded_grad[:, :, offset : offset + span_count]
        )
    return running


def tap_grads(primed_grad, history, margin, span_count):
    columns = []
    for offset in range(margin + 1):
        columns.append(
            jnp.sum(
                primed_grad * history[:, :, margin - offset : margin - offset + span_count], axis=-1
            )
        )
    return jnp.stack(columns, axis=-1)


def packed_tables(length):
    steps = np.arange(length)
    phase = (steps[:, None] * steps[None, :]) % (2 * length)
    angles = np.pi / length * phase
    sines = np.sin(angles)
    sines[:, 0] = 1.0 - 2.0 * (steps % 2)
    table = np.concatenate([np.cos(angles), sines], 1).astype(np.float32)
    high = table.astype(jnp.bfloat16)
    low = (table - high.astype(np.float32)).astype(jnp.bfloat16)
    return np.stack([high, low])


def fused_kernel(
    sizes,
    feat_hbm,
    cot_hbm,
    filt_hbm,
    coef_hbm,
    table_hbm,
    gated_hbm,
    grad_hbm,
    long_hbm,
    small_hbm,
    table,
    coef_rows,
    coef_cols,
    arrived,
    stacked,
    primed_buf,
    freq,
    back_high,
    back_low,
    back_time,
    results,
    sums,
    sums_out,
    load_sem,
    own_in,
    own_out,
    in_send,
    in_recv,
    out_send,
    out_recv,
    small_own,
    small_send,
    small_recv,
):
    groups, rows, span, length, taps, chunks = sizes
    chunk_rows = rows // chunks
    me = lax.axis_index("seq")

    def at(index, extent):
        return pl.ds(pl.multiple_of(index * extent, extent), extent)

    def chan_rows(owner, chunk):
        start = owner * rows + chunk * chunk_rows
        return pl.ds(pl.multiple_of(start, chunk_rows), chunk_rows)

    loads = [
        pltpu.make_async_copy(coef_hbm.at[:, at(me, rows)], coef_rows.at[0:16, :], load_sem.at[0]),
        pltpu.make_async_copy(table_hbm, table, load_sem.at[1]),
    ]
    for load in loads:
        load.start()

    def in_pairs(owner, source, chunk):
        taken = chan_rows(owner, chunk)
        kept = pl.ds(chunk * chunk_rows, chunk_rows)
        tokens = at(source, span)
        return [
            (filt_hbm.at[taken, :], arrived.at[4, kept, tokens]),
            (feat_hbm.at[:, taken, :], arrived.at[0:3, kept, tokens]),
            (cot_hbm.at[taken, :], arrived.at[3, kept, tokens]),
        ]

    def out_pairs(target, owner, chunk):
        kept = pl.ds(chunk * chunk_rows, chunk_rows)
        placed = chan_rows(owner, chunk)
        tokens = at(target, span)
        return [
            (results.at[0, kept, tokens], gated_hbm.at[placed, :]),
            (results.at[1:4, kept, tokens], grad_hbm.at[:, placed, :]),
            (results.at[4, kept, tokens], long_hbm.at[placed, :]),
        ]

    def remote(pair, send_sem, recv_sem, peer):
        return pltpu.make_async_remote_copy(
            src_ref=pair[0],
            dst_ref=pair[1],
            send_sem=send_sem,
            recv_sem=recv_sem,
            device_id={"seq": peer},
            device_id_type=pl.DeviceIdType.MESH,
        )

    own_copies = []
    for chunk in range(chunks):
        for kind, pair in enumerate(in_pairs(me, me, chunk)):
            copy = pltpu.make_async_copy(pair[0], pair[1], own_in.at[chunk, kind])
            copy.start()
            own_copies.append(copy)

    barrier = pltpu.get_barrier_semaphore()
    for offset in range(1, groups):
        pl.semaphore_signal(
            barrier,
            inc=1,
            device_id={"seq": lax.rem(me + offset, groups)},
            device_id_type=pl.DeviceIdType.MESH,
        )
    pl.semaphore_wait(barrier, groups - 1)

    sent = []
    for chunk in range(chunks):
        for offset in range(1, groups):
            peer = lax.rem(me + offset, groups)
            for kind, pair in enumerate(in_pairs(peer, me, chunk)):
                copy = remote(
                    pair, in_send.at[chunk, kind, offset], in_recv.at[chunk, kind, offset], peer
                )
                copy.start()
                sent.append(copy)

    loads[0].wait()
    coef_rows[16:, :] = jnp.zeros((coef_rows.shape[0] - 16, rows), jnp.float32)
    coef_cols[...] = coef_rows[...].T
    loads[1].wait()

    group_rows = 16
    scale = 1.0 / length

    def column(index, picked):
        return coef_cols[picked, index : index + 1]

    def delayed(values, offset):
        if offset == 0:
            return values
        lane = lax.broadcasted_iota(jnp.int32, values.shape, 1)
        return jnp.where(lane >= offset, pltpu.roll(values, offset, 1), 0.0)

    def advanced(values, offset):
        if offset == 0:
            return values
        lane = lax.broadcasted_iota(jnp.int32, values.shape, 1)
        moved = pltpu.roll(values, length - offset, 1)
        return jnp.where(lane < length - offset, moved, 0.0)

    for chunk in range(chunks):
        base = chunk * chunk_rows
        for kind in range(3):
            own_copies[chunk * 3 + kind].wait()
        for offset in range(1, groups):
            source = lax.rem(me + groups - offset, groups)
            for kind, pair in enumerate(in_pairs(me, source, chunk)):
                remote(
                    pair, in_send.at[chunk, kind, offset], in_recv.at[chunk, kind, offset], source
                ).wait_recv()

        @pl.loop(0, chunk_rows // group_rows)
        def _(step):
            inner = pl.ds(pl.multiple_of(step * group_rows, group_rows), group_rows)
            picked = pl.ds(pl.multiple_of(base + step * group_rows, group_rows), group_rows)
            primed = []
            for stream in range(3):
                wide = arrived[stream, picked, :].astype(jnp.float32)
                running = column(stream * taps, picked) * wide
                for offset in range(1, taps):
                    running = running + column(stream * taps + offset, picked) * delayed(
                        wide, offset
                    )
                primed.append(running)
                primed_buf[stream, inner, :] = running
            stacked[0, inner, :] = (primed[1] * primed[2]).astype(jnp.bfloat16)
            cot_wide = arrived[3, picked, :].astype(jnp.float32)
            stacked[1, inner, :] = (cot_wide * primed[0]).astype(jnp.bfloat16)
            stacked[2, inner, :] = arrived[4, picked, :]

        tile = 256

        @pl.loop(0, 2 * length // tile)
        def _(step):
            columns = pl.ds(pl.multiple_of(step * tile, tile), tile)
            left = stacked[...].reshape(3 * chunk_rows, length)
            total = jnp.dot(left, table[0, :, columns], preferred_element_type=jnp.float32)
            total += jnp.dot(left, table[1, :, columns], preferred_element_type=jnp.float32)
            freq[:, :, columns] = total.reshape(3, chunk_rows, tile)

        @pl.loop(0, chunk_rows // group_rows)
        def _(step):
            inner = pl.ds(pl.multiple_of(step * group_rows, group_rows), group_rows)
            first = lax.broadcasted_iota(jnp.int32, (group_rows, length), 1) == 0
            weight = jnp.where(first, 0.5 * scale, scale)
            mix_c, mix_s = freq[0, inner, :length], freq[0, inner, length:]
            grad_c, grad_s = freq[1, inner, :length], freq[1, inner, length:]
            kern_c, kern_s = freq[2, inner, :length], freq[2, inner, length:]

            def put(slot, left_c, left_s, right_c, right_s, sign):
                both = left_s * right_s
                even = left_c * right_c + sign * jnp.where(first, 0.0, both)
                odd = jnp.where(first, both, left_s * right_c - sign * (left_c * right_s))
                for half, part in enumerate((even, odd)):
                    value = part * weight
                    high = value.astype(jnp.bfloat16)
                    low = (value - high.astype(jnp.float32)).astype(jnp.bfloat16)
                    back_high[slot, inner, half * length : (half + 1) * length] = high
                    back_low[slot, inner, half * length : (half + 1) * length] = low

            put(0, mix_c, mix_s, kern_c, kern_s, -1.0)
            put(1, grad_c, grad_s, kern_c, kern_s, 1.0)
            put(2, grad_c, grad_s, mix_c, mix_s, 1.0)

        @pl.loop(0, length // tile)
        def _(step):
            picked = pl.ds(pl.multiple_of(step * tile, tile), tile)
            high = back_high[...].reshape(3 * chunk_rows, 2 * length)
            low = back_low[...].reshape(3 * chunk_rows, 2 * length)
            turned = (((1,), (1,)), ((), ()))
            total = lax.dot_general(
                high, table[0, picked, :], turned, preferred_element_type=jnp.float32
            )
            total += lax.dot_general(
                low, table[0, picked, :], turned, preferred_element_type=jnp.float32
            )
            total += lax.dot_general(
                high, table[1, picked, :], turned, preferred_element_type=jnp.float32
            )
            back_time[:, :, picked] = total.reshape(3, chunk_rows, tile)

        @pl.loop(0, chunk_rows // group_rows)
        def _(step):
            inner = pl.ds(pl.multiple_of(step * group_rows, group_rows), group_rows)
            picked = pl.ds(pl.multiple_of(base + step * group_rows, group_rows), group_rows)
            mixed = stacked[0, inner, :].astype(jnp.float32)
            gated = stacked[1, inner, :].astype(jnp.float32)
            gain = column(3 * taps, picked)
            long_wide = (
                (back_time[0, inner, :] + gain * mixed).astype(jnp.bfloat16).astype(jnp.float32)
            )
            mixed_back = (
                (back_time[1, inner, :] + gain * gated).astype(jnp.bfloat16).astype(jnp.float32)
            )
            results[4, picked, :] = back_time[2, inner, :].astype(jnp.bfloat16)
            results[0, picked, :] = (primed_buf[0, inner, :] * long_wide).astype(jnp.bfloat16)
            cot_wide = arrived[3, picked, :].astype(jnp.float32)
            primed_grad = [
                cot_wide * long_wide,
                mixed_back * primed_buf[2, inner, :],
                mixed_back * primed_buf[1, inner, :],
            ]
            lane = lax.broadcasted_iota(jnp.int32, (group_rows, sums.shape[1]), 1)
            line = jnp.zeros((group_rows, sums.shape[1]), jnp.float32)
            for stream in range(3):
                moving = primed_grad[stream]
                wide = arrived[stream, picked, :].astype(jnp.float32)
                running = column(stream * taps, picked) * moving
                for offset in range(taps):
                    if offset:
                        running = running + column(stream * taps + offset, picked) * advanced(
                            moving, offset
                        )
                    total = jnp.sum(moving * delayed(wide, offset), axis=1, keepdims=True)
                    line = jnp.where(lane == stream * taps + offset, total, line)
                results[1 + stream, picked, :] = running.astype(jnp.bfloat16)
            total = jnp.sum(gated * mixed, axis=1, keepdims=True)
            sums[picked, :] = jnp.where(lane == 3 * taps, total, line)

        for offset in range(1, groups):
            peer = lax.rem(me + offset, groups)
            for kind, pair in enumerate(out_pairs(peer, me, chunk)):
                copy = remote(
                    pair, out_send.at[chunk, kind, offset], out_recv.at[chunk, kind, offset], peer
                )
                copy.start()
                sent.append(copy)
        for kind, pair in enumerate(out_pairs(me, me, chunk)):
            copy = pltpu.make_async_copy(pair[0], pair[1], own_out.at[chunk, kind])
            copy.start()
            own_copies.append(copy)

    sums_out[...] = sums[...].T[0:16, :]
    own_small = pltpu.make_async_copy(sums_out, small_hbm.at[:, at(me, rows)], small_own)
    own_small.start()
    for offset in range(1, groups):
        peer = lax.rem(me + offset, groups)
        copy = remote(
            (sums_out, small_hbm.at[:, at(me, rows)]),
            small_send.at[offset],
            small_recv.at[offset],
            peer,
        )
        copy.start()
        sent.append(copy)
    for copy in sent:
        copy.wait_send()
    for copy in own_copies[3 * chunks :]:
        copy.wait()
    own_small.wait()
    for offset in range(1, groups):
        source = lax.rem(me + groups - offset, groups)
        for chunk in range(chunks):
            for kind, pair in enumerate(out_pairs(me, source, chunk)):
                remote(
                    pair, out_send.at[chunk, kind, offset], out_recv.at[chunk, kind, offset], source
                ).wait_recv()
        remote(
            (sums_out, small_hbm.at[:, at(source, rows)]),
            small_send.at[offset],
            small_recv.at[offset],
            source,
        ).wait_recv()


def fused(features, cotangent, long_filter, short_filters, skip_gain, groups, chunks):
    channels, span = cotangent.shape
    rows = channels // groups
    length = span * groups
    taps = short_filters.shape[2]
    chunk_rows = rows // chunks
    coef = jnp.concatenate(
        [
            jnp.swapaxes(short_filters, 1, 2).reshape(3 * taps, channels),
            skip_gain[None],
            jnp.zeros((15 - 3 * taps, channels), jnp.float32),
        ],
        0,
    )
    hbm = pl.BlockSpec(memory_space=pl.ANY)
    dma = pltpu.SemaphoreType.DMA
    narrow = jnp.bfloat16
    gated_out, feature_grad, long_grad, small = pl.pallas_call(
        functools.partial(fused_kernel, (groups, rows, span, length, taps, chunks)),
        out_shape=(
            jax.ShapeDtypeStruct((channels, span), narrow),
            jax.ShapeDtypeStruct((3, channels, span), narrow),
            jax.ShapeDtypeStruct((channels, span), narrow),
            jax.ShapeDtypeStruct((16, channels), jnp.float32),
        ),
        in_specs=[hbm] * 5,
        out_specs=(hbm,) * 4,
        scratch_shapes=[
            pltpu.VMEM((2, length, 2 * length), narrow),
            pltpu.VMEM((rows, rows), jnp.float32),
            pltpu.VMEM((rows, rows), jnp.float32),
            pltpu.VMEM((5, rows, length), narrow),
            pltpu.VMEM((3, chunk_rows, length), narrow),
            pltpu.VMEM((3, chunk_rows, length), jnp.float32),
            pltpu.VMEM((3, chunk_rows, 2 * length), jnp.float32),
            pltpu.VMEM((3, chunk_rows, 2 * length), narrow),
            pltpu.VMEM((3, chunk_rows, 2 * length), narrow),
            pltpu.VMEM((3, chunk_rows, length), jnp.float32),
            pltpu.VMEM((5, rows, length), narrow),
            pltpu.VMEM((rows, rows), jnp.float32),
            pltpu.VMEM((16, rows), jnp.float32),
            dma((2,)),
            dma((chunks, 3)),
            dma((chunks, 3)),
            dma((chunks, 3, groups)),
            dma((chunks, 3, groups)),
            dma((chunks, 3, groups)),
            dma((chunks, 3, groups)),
            dma,
            dma((groups,)),
            dma((groups,)),
        ],
        compiler_params=pltpu.CompilerParams(
            collective_id=0, has_side_effects=True, vmem_limit_bytes=48 * 1024 * 1024
        ),
    )(features, cotangent, long_filter, coef, packed_tables(length))
    short_grad = jnp.swapaxes(small[: 3 * taps].reshape(3, taps, channels), 1, 2)
    return gated_out, feature_grad, long_grad, short_grad, small[3 * taps]


def dense_fits(features, short_filters, groups):
    channels, span = features.shape[1:]
    rows, length = channels // groups, span * groups
    return (
        channels % groups == 0
        and rows % 128 == 0
        and span % 128 == 0
        and length % 256 == 0
        and length <= 1024
        and rows <= 256
        and 3 * short_filters.shape[2] < 16
    )


def shards(features, cotangent, long_filter, short_filters, skip_gain):
    groups = lax.axis_size("seq")
    if dense_fits(features, short_filters, groups):
        return fused(
            features, cotangent, long_filter, short_filters, skip_gain, groups, chunk_count
        )
    seq_index = lax.axis_index("seq")
    channels = features.shape[1]
    per_group = channels // groups
    margin = short_filters.shape[2] - 1
    local_gain = lax.dynamic_slice_in_dim(skip_gain, seq_index * per_group, per_group, 0)
    stacked = jnp.concatenate([features, cotangent[None], long_filter[None]], 0)
    columns = lax.all_to_all(stacked, "seq", split_axis=1, concat_axis=2, tiled=True)
    weights = lax.dynamic_slice_in_dim(short_filters, seq_index * per_group, per_group, 1)
    length = columns.shape[2]
    history = jnp.pad(columns[:3].astype(jnp.float32), ((0, 0), (0, 0), (margin, 0)))
    primed = featurize(history, weights, margin, length)
    mixed_term = (primed[1] * primed[2]).astype(jnp.bfloat16)
    cot_wide = columns[3].astype(jnp.float32)
    gated_grad = (cot_wide * primed[0]).astype(jnp.bfloat16)
    long_out, mixed_grad, kernel_grad = spectral(mixed_term, gated_grad, columns[4], local_gain)
    long_wide = long_out.astype(jnp.float32)
    mixed_back = mixed_grad.astype(jnp.float32)
    gated_out = (primed[0] * long_wide).astype(jnp.bfloat16)
    primed_grad = jnp.stack([cot_wide * long_wide, mixed_back * primed[2], mixed_back * primed[1]])
    padded_grad = jnp.pad(primed_grad, ((0, 0), (0, 0), (0, margin)))
    feature_grad = unfeaturize(padded_grad, weights, length).astype(jnp.bfloat16)
    taps_grad = tap_grads(primed_grad, history, margin, length)
    gain_grad = jnp.sum(gated_grad.astype(jnp.float32) * mixed_term.astype(jnp.float32), axis=-1)
    results = jnp.concatenate([gated_out[None], feature_grad, kernel_grad[None]], 0)
    row_blocks = lax.all_to_all(results, "seq", split_axis=2, concat_axis=1, tiled=True)
    short_grad, skip_grad = (
        lax.all_gather(taps_grad, "seq", axis=1, tiled=True),
        lax.all_gather(gain_grad, "seq", axis=0, tiled=True),
    )
    return (row_blocks[0], row_blocks[1:4], row_blocks[4], short_grad, skip_grad)


def solution(mesh):
    placed = (
        P(None, "chan", "seq"),
        P("chan", "seq"),
        P("chan", "seq"),
        P(None, "chan", None),
        P("chan"),
    )
    return jax.shard_map(
        shards,
        mesh=mesh,
        in_specs=placed,
        out_specs=(
            P("chan", "seq"),
            P(None, "chan", "seq"),
            P("chan", "seq"),
            P(None, "chan", None),
            P("chan"),
        ),
        check_vma=False,
    )
```

```python
import functools
import math

import jax
import jax.numpy as jnp
import numpy as np
from jax import lax
from jax.experimental import pallas as pl
from jax.experimental.pallas import tpu as pltpu
from jax.sharding import PartitionSpec as P

inner_length = 128
radix_width = 8
chunk_count = 2


def phase_tables(row_count, col_count, length, direction):
    phase_index = (
        lax.iota(jnp.int32, row_count)[:, None] * lax.iota(jnp.int32, col_count)[None, :] % length
    )
    angles = direction * 2.0 * math.pi / length * phase_index.astype(jnp.float32)
    return (jnp.cos(angles), jnp.sin(angles))


def last_axis(operand, matrix):
    return jnp.einsum("...n,nk->...k", operand, matrix, precision=lax.Precision.HIGH)


def first_axis(operand, matrix):
    return jnp.einsum("...ab,ak->...kb", operand, matrix, precision=lax.Precision.HIGH)


def transform(real_part, imag_part, direction):
    length = real_part.shape[-1]
    if length <= inner_length or length % radix_width != 0:
        cos_table, sin_table = phase_tables(length, length, length, direction)
        return (
            last_axis(real_part, cos_table) - last_axis(imag_part, sin_table),
            last_axis(real_part, sin_table) + last_axis(imag_part, cos_table),
        )
    rest_length = length // radix_width
    grid_shape = real_part.shape[:-1] + (radix_width, rest_length)
    real_grid = real_part.reshape(grid_shape)
    imag_grid = imag_part.reshape(grid_shape)
    cos_table, sin_table = phase_tables(radix_width, radix_width, radix_width, direction)
    section_real = first_axis(real_grid, cos_table) - first_axis(imag_grid, sin_table)
    section_imag = first_axis(real_grid, sin_table) + first_axis(imag_grid, cos_table)
    twist_cos, twist_sin = phase_tables(radix_width, rest_length, length, direction)
    turned_real = section_real * twist_cos - section_imag * twist_sin
    turned_imag = section_real * twist_sin + section_imag * twist_cos
    inner_real, inner_imag = transform(turned_real, turned_imag, direction)
    return (
        jnp.swapaxes(inner_real, -1, -2).reshape(real_part.shape),
        jnp.swapaxes(inner_imag, -1, -2).reshape(real_part.shape),
    )


def spectral(mixed_term, gated_grad, kernel, local_gain):
    length = mixed_term.shape[-1]
    mixed_wide = mixed_term.astype(jnp.float32)
    gated_wide = gated_grad.astype(jnp.float32)
    kernel_wide = kernel.astype(jnp.float32)
    extend = ((0, 0), (0, length))
    real_in = jnp.stack([jnp.pad(mixed_wide, extend), jnp.pad(kernel_wide, extend)])
    imag_in = jnp.stack(
        [jnp.pad(gated_wide, extend), jnp.zeros((kernel_wide.shape[0], 2 * length), jnp.float32)]
    )
    freq_real, freq_imag = transform(real_in, imag_in, -1.0)
    packed_real = freq_real[0]
    packed_imag = freq_imag[0]
    mirror_real = jnp.roll(jnp.flip(packed_real, -1), 1, -1)
    mirror_imag = jnp.roll(jnp.flip(packed_imag, -1), 1, -1)
    mix_real = 0.5 * (packed_real + mirror_real)
    mix_imag = 0.5 * (packed_imag - mirror_imag)
    grad_real = 0.5 * (packed_imag + mirror_imag)
    grad_imag = 0.5 * (mirror_real - packed_real)
    kern_real = freq_real[1]
    kern_imag = freq_imag[1]
    conv_real = mix_real * kern_real - mix_imag * kern_imag
    conv_imag = mix_real * kern_imag + mix_imag * kern_real
    corr_real = grad_real * kern_real + grad_imag * kern_imag
    corr_imag = grad_imag * kern_real - grad_real * kern_imag
    cross_real = grad_real * mix_real + grad_imag * mix_imag
    cross_imag = grad_imag * mix_real - grad_real * mix_imag
    back_real = jnp.stack([conv_real - corr_imag, cross_real])
    back_imag = jnp.stack([conv_imag + corr_real, cross_imag])
    time_real, time_imag = transform(back_real, back_imag, 1.0)
    inverse_scale = 1.0 / (2 * length)
    conv_part = time_real[0, :, :length] * inverse_scale
    corr_part = time_imag[0, :, :length] * inverse_scale
    cross_part = time_real[1, :, :length] * inverse_scale
    gain_column = local_gain[:, None]
    long_out = (conv_part + gain_column * mixed_wide).astype(jnp.bfloat16)
    mixed_grad = (corr_part + gain_column * gated_wide).astype(jnp.bfloat16)
    return (long_out, mixed_grad, cross_part.astype(jnp.bfloat16))


def featurize(history, weights, margin, span_count):
    running = weights[:, :, 0:1] * history[:, :, margin : margin + span_count]
    for offset in range(1, margin + 1):
        running = (
            running
            + weights[:, :, offset : offset + 1]
            * history[:, :, margin - offset : margin - offset + span_count]
        )
    return running


def unfeaturize(padded_grad, weights, span_count):
    running = weights[:, :, 0:1] * padded_grad[:, :, 0:span_count]
    for offset in range(1, weights.shape[2]):
        running = (
            running
            + weights[:, :, offset : offset + 1] * padded_grad[:, :, offset : offset + span_count]
        )
    return running


def tap_grads(primed_grad, history, margin, span_count):
    columns = []
    for offset in range(margin + 1):
        columns.append(
            jnp.sum(
                primed_grad * history[:, :, margin - offset : margin - offset + span_count], axis=-1
            )
        )
    return jnp.stack(columns, axis=-1)


def packed_tables(length):
    steps = np.arange(length)
    phase = (steps[:, None] * steps[None, :]) % (2 * length)
    angles = np.pi / length * phase
    sines = np.sin(angles)
    sines[:, 0] = 1.0 - 2.0 * (steps % 2)
    table = np.concatenate([np.cos(angles), sines], 1).astype(np.float32)
    high = table.astype(jnp.bfloat16)
    low = (table - high.astype(np.float32)).astype(jnp.bfloat16)
    return np.stack([high, low])


def fused_kernel(
    sizes,
    feat_hbm,
    cot_hbm,
    filt_hbm,
    short_hbm,
    gain_hbm,
    table_hbm,
    gated_hbm,
    grad_hbm,
    long_hbm,
    taps_hbm,
    skip_hbm,
    table,
    short_rows,
    gain_line,
    coef_rows,
    coef_cols,
    arrived,
    stacked,
    primed_buf,
    freq,
    back_high,
    back_low,
    back_time,
    results,
    sums,
    taps_out,
    skip_out,
    load_sem,
    own_in,
    own_out,
    in_send,
    in_recv,
    out_send,
    out_recv,
    small_own,
    small_send,
    small_recv,
):
    groups, rows, span, length, taps, chunks = sizes
    chunk_rows = rows // chunks
    me = lax.axis_index("seq")

    def at(index, extent):
        return pl.ds(pl.multiple_of(index * extent, extent), extent)

    def chan_rows(owner, chunk):
        start = owner * rows + chunk * chunk_rows
        return pl.ds(pl.multiple_of(start, chunk_rows), chunk_rows)

    loads = [
        pltpu.make_async_copy(short_hbm.at[:, :, at(me, rows)], short_rows, load_sem.at[0]),
        pltpu.make_async_copy(gain_hbm, gain_line, load_sem.at[1]),
        pltpu.make_async_copy(table_hbm, table, load_sem.at[2]),
    ]
    for load in loads:
        load.start()

    def in_pairs(owner, source, chunk):
        taken = chan_rows(owner, chunk)
        kept = pl.ds(chunk * chunk_rows, chunk_rows)
        return [
            (filt_hbm.at[taken, :], arrived.at[source, 4, kept, :]),
            (feat_hbm.at[:, taken, :], arrived.at[source, 0:3, kept, :]),
            (cot_hbm.at[taken, :], arrived.at[source, 3, kept, :]),
        ]

    def out_pairs(target, owner, chunk):
        kept = pl.ds(chunk * chunk_rows, chunk_rows)
        placed = chan_rows(owner, chunk)
        return [
            (results.at[target, 0, kept, :], gated_hbm.at[placed, :]),
            (results.at[target, 1:4, kept, :], grad_hbm.at[:, placed, :]),
            (results.at[target, 4, kept, :], long_hbm.at[placed, :]),
        ]

    def remote(pair, send_sem, recv_sem, peer):
        return pltpu.make_async_remote_copy(
            src_ref=pair[0],
            dst_ref=pair[1],
            send_sem=send_sem,
            recv_sem=recv_sem,
            device_id={"seq": peer},
            device_id_type=pl.DeviceIdType.MESH,
        )

    own_copies = []
    for chunk in range(chunks):
        for kind, pair in enumerate(in_pairs(me, me, chunk)):
            copy = pltpu.make_async_copy(pair[0], pair[1], own_in.at[chunk, kind])
            copy.start()
            own_copies.append(copy)

    barrier = pltpu.get_barrier_semaphore()
    for offset in range(1, groups):
        pl.semaphore_signal(
            barrier,
            inc=1,
            device_id={"seq": lax.rem(me + offset, groups)},
            device_id_type=pl.DeviceIdType.MESH,
        )
    pl.semaphore_wait(barrier, groups - 1)

    sent = []
    for chunk in range(chunks):
        for offset in range(1, groups):
            peer = lax.rem(me + offset, groups)
            for kind, pair in enumerate(in_pairs(peer, me, chunk)):
                copy = remote(
                    pair, in_send.at[chunk, kind, offset], in_recv.at[chunk, kind, offset], peer
                )
                copy.start()
                sent.append(copy)

    loads[0].wait()
    loads[1].wait()
    coef_rows[...] = jnp.zeros_like(coef_rows)
    for stream in range(3):
        coef_rows[stream * taps : (stream + 1) * taps, :] = short_rows[stream]
    gain_row = jnp.zeros((1, rows), jnp.float32)
    for group in range(groups):
        part = gain_line[:, group * rows : (group + 1) * rows]
        gain_row = gain_row + jnp.where(me == group, part, 0.0)
    coef_rows[3 * taps : 3 * taps + 1, :] = gain_row
    coef_cols[...] = coef_rows[...].T
    loads[2].wait()

    group_rows = 64
    scale = 1.0 / length

    def tokens_of(kind, picked):
        return jnp.concatenate([arrived[group, kind, picked, :] for group in range(groups)], 1)

    def finish(kind, picked, values):
        for group in range(groups):
            results[group, kind, picked, :] = values[:, group * span : (group + 1) * span].astype(
                jnp.bfloat16
            )

    def column(index, picked):
        return coef_cols[picked, index : index + 1]

    def delayed(values, offset):
        if offset == 0:
            return values
        lane = lax.broadcasted_iota(jnp.int32, values.shape, 1)
        return jnp.where(lane >= offset, pltpu.roll(values, offset, 1), 0.0)

    def advanced(values, offset):
        if offset == 0:
            return values
        lane = lax.broadcasted_iota(jnp.int32, values.shape, 1)
        moved = pltpu.roll(values, length - offset, 1)
        return jnp.where(lane < length - offset, moved, 0.0)

    for chunk in range(chunks):
        base = chunk * chunk_rows
        for kind in range(3):
            own_copies[chunk * 3 + kind].wait()
        for offset in range(1, groups):
            source = lax.rem(me + groups - offset, groups)
            for kind, pair in enumerate(in_pairs(me, source, chunk)):
                remote(
                    pair, in_send.at[chunk, kind, offset], in_recv.at[chunk, kind, offset], source
                ).wait_recv()

        @pl.loop(0, chunk_rows // group_rows)
        def _(step):
            inner = pl.ds(pl.multiple_of(step * group_rows, group_rows), group_rows)
            picked = pl.ds(pl.multiple_of(base + step * group_rows, group_rows), group_rows)
            primed = []
            for stream in range(3):
                wide = tokens_of(stream, picked).astype(jnp.float32)
                running = column(stream * taps, picked) * wide
                for offset in range(1, taps):
                    running = running + column(stream * taps + offset, picked) * delayed(
                        wide, offset
                    )
                primed.append(running)
                primed_buf[stream, inner, :] = running
            stacked[0, inner, :] = (primed[1] * primed[2]).astype(jnp.bfloat16)
            cot_wide = tokens_of(3, picked).astype(jnp.float32)
            stacked[1, inner, :] = (cot_wide * primed[0]).astype(jnp.bfloat16)
            stacked[2, inner, :] = tokens_of(4, picked)

        tile = 256

        @pl.loop(0, 2 * length // tile)
        def _(step):
            columns = pl.ds(pl.multiple_of(step * tile, tile), tile)
            left = stacked[...].reshape(3 * chunk_rows, length)
            total = jnp.dot(left, table[0, :, columns], preferred_element_type=jnp.float32)
            total += jnp.dot(left, table[1, :, columns], preferred_element_type=jnp.float32)
            freq[:, :, columns] = total.reshape(3, chunk_rows, tile)

        @pl.loop(0, chunk_rows // group_rows)
        def _(step):
            inner = pl.ds(pl.multiple_of(step * group_rows, group_rows), group_rows)
            first = lax.broadcasted_iota(jnp.int32, (group_rows, length), 1) == 0
            weight = jnp.where(first, 0.5 * scale, scale)
            mix_c, mix_s = freq[0, inner, :length], freq[0, inner, length:]
            grad_c, grad_s = freq[1, inner, :length], freq[1, inner, length:]
            kern_c, kern_s = freq[2, inner, :length], freq[2, inner, length:]

            def put(slot, left_c, left_s, right_c, right_s, sign):
                both = left_s * right_s
                even = left_c * right_c + sign * jnp.where(first, 0.0, both)
                odd = jnp.where(first, both, left_s * right_c - sign * (left_c * right_s))
                for half, part in enumerate((even, odd)):
                    value = part * weight
                    high = value.astype(jnp.bfloat16)
                    low = (value - high.astype(jnp.float32)).astype(jnp.bfloat16)
                    back_high[slot, inner, half * length : (half + 1) * length] = high
                    back_low[slot, inner, half * length : (half + 1) * length] = low

            put(0, mix_c, mix_s, kern_c, kern_s, -1.0)
            put(1, grad_c, grad_s, kern_c, kern_s, 1.0)
            put(2, grad_c, grad_s, mix_c, mix_s, 1.0)

        @pl.loop(0, length // tile)
        def _(step):
            picked = pl.ds(pl.multiple_of(step * tile, tile), tile)
            high = back_high[...].reshape(3 * chunk_rows, 2 * length)
            low = back_low[...].reshape(3 * chunk_rows, 2 * length)
            turned = (((1,), (1,)), ((), ()))
            total = lax.dot_general(
                high, table[0, picked, :], turned, preferred_element_type=jnp.float32
            )
            total += lax.dot_general(
                low, table[0, picked, :], turned, preferred_element_type=jnp.float32
            )
            total += lax.dot_general(
                high, table[1, picked, :], turned, preferred_element_type=jnp.float32
            )
            back_time[:, :, picked] = total.reshape(3, chunk_rows, tile)

        @pl.loop(0, chunk_rows // group_rows)
        def _(step):
            inner = pl.ds(pl.multiple_of(step * group_rows, group_rows), group_rows)
            picked = pl.ds(pl.multiple_of(base + step * group_rows, group_rows), group_rows)
            mixed = stacked[0, inner, :].astype(jnp.float32)
            gated = stacked[1, inner, :].astype(jnp.float32)
            gain = column(3 * taps, picked)
            long_wide = (
                (back_time[0, inner, :] + gain * mixed).astype(jnp.bfloat16).astype(jnp.float32)
            )
            mixed_back = (
                (back_time[1, inner, :] + gain * gated).astype(jnp.bfloat16).astype(jnp.float32)
            )
            finish(4, picked, back_time[2, inner, :])
            finish(0, picked, primed_buf[0, inner, :] * long_wide)
            cot_wide = tokens_of(3, picked).astype(jnp.float32)
            primed_grad = [
                cot_wide * long_wide,
                mixed_back * primed_buf[2, inner, :],
                mixed_back * primed_buf[1, inner, :],
            ]
            lane = lax.broadcasted_iota(jnp.int32, (group_rows, sums.shape[1]), 1)
            line = jnp.zeros((group_rows, sums.shape[1]), jnp.float32)
            for stream in range(3):
                moving = primed_grad[stream]
                wide = tokens_of(stream, picked).astype(jnp.float32)
                running = column(stream * taps, picked) * moving
                for offset in range(taps):
                    if offset:
                        running = running + column(stream * taps + offset, picked) * advanced(
                            moving, offset
                        )
                    total = jnp.sum(moving * delayed(wide, offset), axis=1, keepdims=True)
                    line = jnp.where(lane == stream * taps + offset, total, line)
                finish(1 + stream, picked, running)
            total = jnp.sum(gated * mixed, axis=1, keepdims=True)
            sums[picked, :] = jnp.where(lane == 3 * taps, total, line)

        for offset in range(1, groups):
            peer = lax.rem(me + offset, groups)
            for kind, pair in enumerate(out_pairs(peer, me, chunk)):
                copy = remote(
                    pair, out_send.at[chunk, kind, offset], out_recv.at[chunk, kind, offset], peer
                )
                copy.start()
                sent.append(copy)
        for kind, pair in enumerate(out_pairs(me, me, chunk)):
            copy = pltpu.make_async_copy(pair[0], pair[1], own_out.at[chunk, kind])
            copy.start()
            own_copies.append(copy)

    turned_sums = sums[...].T
    for stream in range(3):
        taps_out[stream] = turned_sums[stream * taps : (stream + 1) * taps, :]
    skip_out[...] = turned_sums[3 * taps : 3 * taps + 1, :]

    def small_pairs(owner):
        return [
            (taps_out, taps_hbm.at[:, :, at(owner, rows)]),
            (skip_out, skip_hbm.at[:, at(owner, rows)]),
        ]

    for kind, pair in enumerate(small_pairs(me)):
        copy = pltpu.make_async_copy(pair[0], pair[1], small_own.at[kind])
        copy.start()
        own_copies.append(copy)
        for offset in range(1, groups):
            peer = lax.rem(me + offset, groups)
            copy = remote(pair, small_send.at[kind, offset], small_recv.at[kind, offset], peer)
            copy.start()
            sent.append(copy)
    for copy in sent:
        copy.wait_send()
    for copy in own_copies[3 * chunks :]:
        copy.wait()
    for offset in range(1, groups):
        source = lax.rem(me + groups - offset, groups)
        for chunk in range(chunks):
            for kind, pair in enumerate(out_pairs(me, source, chunk)):
                remote(
                    pair, out_send.at[chunk, kind, offset], out_recv.at[chunk, kind, offset], source
                ).wait_recv()
        for kind, pair in enumerate(small_pairs(source)):
            remote(
                pair, small_send.at[kind, offset], small_recv.at[kind, offset], source
            ).wait_recv()


def fused(features, cotangent, long_filter, short_filters, skip_gain, groups, chunks):
    channels, span = cotangent.shape
    rows = channels // groups
    length = span * groups
    taps = short_filters.shape[2]
    chunk_rows = rows // chunks
    hbm = pl.BlockSpec(memory_space=pltpu.HBM)
    dma = pltpu.SemaphoreType.DMA
    narrow = jnp.bfloat16
    gated_out, feature_grad, long_grad, taps_grad, gain_grad = pl.pallas_call(
        functools.partial(fused_kernel, (groups, rows, span, length, taps, chunks)),
        out_shape=(
            jax.ShapeDtypeStruct((channels, span), narrow),
            jax.ShapeDtypeStruct((3, channels, span), narrow),
            jax.ShapeDtypeStruct((channels, span), narrow),
            jax.ShapeDtypeStruct((3, taps, channels), jnp.float32),
            jax.ShapeDtypeStruct((1, channels), jnp.float32),
        ),
        in_specs=[hbm] * 6,
        out_specs=(hbm,) * 5,
        scratch_shapes=[
            pltpu.VMEM((2, length, 2 * length), narrow),
            pltpu.VMEM((3, taps, rows), jnp.float32),
            pltpu.VMEM((1, channels), jnp.float32),
            pltpu.VMEM((rows, rows), jnp.float32),
            pltpu.VMEM((rows, rows), jnp.float32),
            pltpu.VMEM((groups, 5, rows, span), narrow),
            pltpu.VMEM((3, chunk_rows, length), narrow),
            pltpu.VMEM((3, chunk_rows, length), jnp.float32),
            pltpu.VMEM((3, chunk_rows, 2 * length), jnp.float32),
            pltpu.VMEM((3, chunk_rows, 2 * length), narrow),
            pltpu.VMEM((3, chunk_rows, 2 * length), narrow),
            pltpu.VMEM((3, chunk_rows, length), jnp.float32),
            pltpu.VMEM((groups, 5, rows, span), narrow),
            pltpu.VMEM((rows, rows), jnp.float32),
            pltpu.VMEM((3, taps, rows), jnp.float32),
            pltpu.VMEM((1, rows), jnp.float32),
            dma((3,)),
            dma((chunks, 3)),
            dma((chunks, 3)),
            dma((chunks, 3, groups)),
            dma((chunks, 3, groups)),
            dma((chunks, 3, groups)),
            dma((chunks, 3, groups)),
            dma((2,)),
            dma((2, groups)),
            dma((2, groups)),
        ],
        compiler_params=pltpu.CompilerParams(
            collective_id=0, has_side_effects=True
        ),
    )(
        features,
        cotangent,
        long_filter,
        jnp.swapaxes(short_filters, 1, 2),
        skip_gain[None],
        packed_tables(length),
    )
    return gated_out, feature_grad, long_grad, jnp.swapaxes(taps_grad, 1, 2), gain_grad[0]


def dense_fits(features, short_filters, groups):
    channels, span = features.shape[1:]
    rows, length = channels // groups, span * groups
    return (
        channels % groups == 0
        and rows % 128 == 0
        and span % 128 == 0
        and length % 256 == 0
        and length <= 1024
        and rows <= 256
        and 3 * short_filters.shape[2] < 16
    )


def shards(features, cotangent, long_filter, short_filters, skip_gain):
    groups = lax.axis_size("seq")
    if dense_fits(features, short_filters, groups):
        return fused(
            features, cotangent, long_filter, short_filters, skip_gain, groups, chunk_count
        )
    seq_index = lax.axis_index("seq")
    channels = features.shape[1]
    per_group = channels // groups
    margin = short_filters.shape[2] - 1
    local_gain = lax.dynamic_slice_in_dim(skip_gain, seq_index * per_group, per_group, 0)
    stacked = jnp.concatenate([features, cotangent[None], long_filter[None]], 0)
    columns = lax.all_to_all(stacked, "seq", split_axis=1, concat_axis=2, tiled=True)
    weights = lax.dynamic_slice_in_dim(short_filters, seq_index * per_group, per_group, 1)
    length = columns.shape[2]
    history = jnp.pad(columns[:3].astype(jnp.float32), ((0, 0), (0, 0), (margin, 0)))
    primed = featurize(history, weights, margin, length)
    mixed_term = (primed[1] * primed[2]).astype(jnp.bfloat16)
    cot_wide = columns[3].astype(jnp.float32)
    gated_grad = (cot_wide * primed[0]).astype(jnp.bfloat16)
    long_out, mixed_grad, kernel_grad = spectral(mixed_term, gated_grad, columns[4], local_gain)
    long_wide = long_out.astype(jnp.float32)
    mixed_back = mixed_grad.astype(jnp.float32)
    gated_out = (primed[0] * long_wide).astype(jnp.bfloat16)
    primed_grad = jnp.stack([cot_wide * long_wide, mixed_back * primed[2], mixed_back * primed[1]])
    padded_grad = jnp.pad(primed_grad, ((0, 0), (0, 0), (0, margin)))
    feature_grad = unfeaturize(padded_grad, weights, length).astype(jnp.bfloat16)
    taps_grad = tap_grads(primed_grad, history, margin, length)
    gain_grad = jnp.sum(gated_grad.astype(jnp.float32) * mixed_term.astype(jnp.float32), axis=-1)
    results = jnp.concatenate([gated_out[None], feature_grad, kernel_grad[None]], 0)
    row_blocks = lax.all_to_all(results, "seq", split_axis=2, concat_axis=1, tiled=True)
    short_grad, skip_grad = (
        lax.all_gather(taps_grad, "seq", axis=1, tiled=True),
        lax.all_gather(gain_grad, "seq", axis=0, tiled=True),
    )
    return (row_blocks[0], row_blocks[1:4], row_blocks[4], short_grad, skip_grad)


def solution(mesh):
    placed = (
        P(None, "chan", "seq"),
        P("chan", "seq"),
        P("chan", "seq"),
        P(None, "chan", None),
        P("chan"),
    )
    return jax.shard_map(
        shards,
        mesh=mesh,
        in_specs=placed,
        out_specs=(
            P("chan", "seq"),
            P(None, "chan", "seq"),
            P("chan", "seq"),
            P(None, "chan", None),
            P("chan"),
        ),
        check_vma=False,
    )
```

```python
import functools
import math

import jax
import jax.numpy as jnp
import numpy as np
from jax import lax
from jax.experimental import pallas as pl
from jax.experimental.pallas import tpu as pltpu
from jax.sharding import PartitionSpec as P

inner_length = 128
radix_width = 8
chunk_count = 2


def phase_tables(row_count, col_count, length, direction):
    phase_index = (
        lax.iota(jnp.int32, row_count)[:, None] * lax.iota(jnp.int32, col_count)[None, :] % length
    )
    angles = direction * 2.0 * math.pi / length * phase_index.astype(jnp.float32)
    return (jnp.cos(angles), jnp.sin(angles))


def last_axis(operand, matrix):
    return jnp.einsum("...n,nk->...k", operand, matrix, precision=lax.Precision.HIGH)


def first_axis(operand, matrix):
    return jnp.einsum("...ab,ak->...kb", operand, matrix, precision=lax.Precision.HIGH)


def transform(real_part, imag_part, direction):
    length = real_part.shape[-1]
    if length <= inner_length or length % radix_width != 0:
        cos_table, sin_table = phase_tables(length, length, length, direction)
        return (
            last_axis(real_part, cos_table) - last_axis(imag_part, sin_table),
            last_axis(real_part, sin_table) + last_axis(imag_part, cos_table),
        )
    rest_length = length // radix_width
    grid_shape = real_part.shape[:-1] + (radix_width, rest_length)
    real_grid = real_part.reshape(grid_shape)
    imag_grid = imag_part.reshape(grid_shape)
    cos_table, sin_table = phase_tables(radix_width, radix_width, radix_width, direction)
    section_real = first_axis(real_grid, cos_table) - first_axis(imag_grid, sin_table)
    section_imag = first_axis(real_grid, sin_table) + first_axis(imag_grid, cos_table)
    twist_cos, twist_sin = phase_tables(radix_width, rest_length, length, direction)
    turned_real = section_real * twist_cos - section_imag * twist_sin
    turned_imag = section_real * twist_sin + section_imag * twist_cos
    inner_real, inner_imag = transform(turned_real, turned_imag, direction)
    return (
        jnp.swapaxes(inner_real, -1, -2).reshape(real_part.shape),
        jnp.swapaxes(inner_imag, -1, -2).reshape(real_part.shape),
    )


def spectral(mixed_term, gated_grad, kernel, local_gain):
    length = mixed_term.shape[-1]
    mixed_wide = mixed_term.astype(jnp.float32)
    gated_wide = gated_grad.astype(jnp.float32)
    kernel_wide = kernel.astype(jnp.float32)
    extend = ((0, 0), (0, length))
    real_in = jnp.stack([jnp.pad(mixed_wide, extend), jnp.pad(kernel_wide, extend)])
    imag_in = jnp.stack(
        [jnp.pad(gated_wide, extend), jnp.zeros((kernel_wide.shape[0], 2 * length), jnp.float32)]
    )
    freq_real, freq_imag = transform(real_in, imag_in, -1.0)
    packed_real = freq_real[0]
    packed_imag = freq_imag[0]
    mirror_real = jnp.roll(jnp.flip(packed_real, -1), 1, -1)
    mirror_imag = jnp.roll(jnp.flip(packed_imag, -1), 1, -1)
    mix_real = 0.5 * (packed_real + mirror_real)
    mix_imag = 0.5 * (packed_imag - mirror_imag)
    grad_real = 0.5 * (packed_imag + mirror_imag)
    grad_imag = 0.5 * (mirror_real - packed_real)
    kern_real = freq_real[1]
    kern_imag = freq_imag[1]
    conv_real = mix_real * kern_real - mix_imag * kern_imag
    conv_imag = mix_real * kern_imag + mix_imag * kern_real
    corr_real = grad_real * kern_real + grad_imag * kern_imag
    corr_imag = grad_imag * kern_real - grad_real * kern_imag
    cross_real = grad_real * mix_real + grad_imag * mix_imag
    cross_imag = grad_imag * mix_real - grad_real * mix_imag
    back_real = jnp.stack([conv_real - corr_imag, cross_real])
    back_imag = jnp.stack([conv_imag + corr_real, cross_imag])
    time_real, time_imag = transform(back_real, back_imag, 1.0)
    inverse_scale = 1.0 / (2 * length)
    conv_part = time_real[0, :, :length] * inverse_scale
    corr_part = time_imag[0, :, :length] * inverse_scale
    cross_part = time_real[1, :, :length] * inverse_scale
    gain_column = local_gain[:, None]
    long_out = (conv_part + gain_column * mixed_wide).astype(jnp.bfloat16)
    mixed_grad = (corr_part + gain_column * gated_wide).astype(jnp.bfloat16)
    return (long_out, mixed_grad, cross_part.astype(jnp.bfloat16))


def featurize(history, weights, margin, span_count):
    running = weights[:, :, 0:1] * history[:, :, margin : margin + span_count]
    for offset in range(1, margin + 1):
        running = (
            running
            + weights[:, :, offset : offset + 1]
            * history[:, :, margin - offset : margin - offset + span_count]
        )
    return running


def unfeaturize(padded_grad, weights, span_count):
    running = weights[:, :, 0:1] * padded_grad[:, :, 0:span_count]
    for offset in range(1, weights.shape[2]):
        running = (
            running
            + weights[:, :, offset : offset + 1] * padded_grad[:, :, offset : offset + span_count]
        )
    return running


def tap_grads(primed_grad, history, margin, span_count):
    columns = []
    for offset in range(margin + 1):
        columns.append(
            jnp.sum(
                primed_grad * history[:, :, margin - offset : margin - offset + span_count], axis=-1
            )
        )
    return jnp.stack(columns, axis=-1)


def packed_tables(length):
    steps = np.arange(length)
    phase = (steps[:, None] * steps[None, :]) % (2 * length)
    angles = np.pi / length * phase
    sines = np.sin(angles)
    sines[:, 0] = 1.0 - 2.0 * (steps % 2)
    table = np.concatenate([np.cos(angles), sines], 1).astype(np.float32)
    high = table.astype(jnp.bfloat16)
    low = (table - high.astype(np.float32)).astype(jnp.bfloat16)
    return np.stack([high, low])


def fused_kernel(
    sizes,
    feat_hbm,
    cot_hbm,
    filt_hbm,
    short_hbm,
    gain_hbm,
    table_hbm,
    gated_hbm,
    grad_hbm,
    long_hbm,
    taps_hbm,
    skip_hbm,
    table,
    short_rows,
    gain_line,
    coef_rows,
    coef_cols,
    arrived,
    stacked,
    primed_buf,
    freq,
    back_high,
    back_low,
    back_time,
    results,
    sums,
    taps_out,
    skip_out,
    load_sem,
    own_in,
    own_out,
    in_send,
    in_recv,
    out_send,
    out_recv,
    small_own,
    small_send,
    small_recv,
):
    groups, rows, span, length, taps, chunks = sizes
    chunk_rows = rows // chunks
    me = lax.axis_index("seq")

    def at(index, extent):
        return pl.ds(pl.multiple_of(index * extent, extent), extent)

    def chan_rows(owner, chunk):
        start = owner * rows + chunk * chunk_rows
        return pl.ds(pl.multiple_of(start, chunk_rows), chunk_rows)

    loads = [
        pltpu.make_async_copy(short_hbm.at[:, :, at(me, rows)], short_rows, load_sem.at[0]),
        pltpu.make_async_copy(gain_hbm, gain_line, load_sem.at[1]),
        pltpu.make_async_copy(table_hbm, table, load_sem.at[2]),
    ]
    for load in loads:
        load.start()

    def in_pairs(owner, source, chunk):
        taken = chan_rows(owner, chunk)
        kept = pl.ds(chunk * chunk_rows, chunk_rows)
        return [
            (filt_hbm.at[taken, :], arrived.at[source, 4, kept, :]),
            (feat_hbm.at[:, taken, :], arrived.at[source, 0:3, kept, :]),
            (cot_hbm.at[taken, :], arrived.at[source, 3, kept, :]),
        ]

    def out_pairs(target, owner, chunk):
        kept = pl.ds(chunk * chunk_rows, chunk_rows)
        placed = chan_rows(owner, chunk)
        return [
            (results.at[target, 0, kept, :], gated_hbm.at[placed, :]),
            (results.at[target, 1:4, kept, :], grad_hbm.at[:, placed, :]),
            (results.at[target, 4, kept, :], long_hbm.at[placed, :]),
        ]

    def remote(pair, send_sem, recv_sem, peer):
        return pltpu.make_async_remote_copy(
            src_ref=pair[0],
            dst_ref=pair[1],
            send_sem=send_sem,
            recv_sem=recv_sem,
            device_id={"seq": peer},
            device_id_type=pl.DeviceIdType.MESH,
        )

    own_copies = []
    for chunk in range(chunks):
        for kind, pair in enumerate(in_pairs(me, me, chunk)):
            copy = pltpu.make_async_copy(pair[0], pair[1], own_in.at[chunk, kind])
            copy.start()
            own_copies.append(copy)

    barrier = pltpu.get_barrier_semaphore()
    for offset in range(1, groups):
        pl.semaphore_signal(
            barrier,
            inc=1,
            device_id={"seq": lax.rem(me + offset, groups)},
            device_id_type=pl.DeviceIdType.MESH,
        )
    pl.semaphore_wait(barrier, groups - 1)

    sent = []
    for chunk in range(chunks):
        for offset in range(1, groups):
            peer = lax.rem(me + offset, groups)
            for kind, pair in enumerate(in_pairs(peer, me, chunk)):
                copy = remote(
                    pair, in_send.at[chunk, kind, offset], in_recv.at[chunk, kind, offset], peer
                )
                copy.start()
                sent.append(copy)

    loads[0].wait()
    loads[1].wait()
    coef_rows[...] = jnp.zeros_like(coef_rows)
    for stream in range(3):
        coef_rows[stream * taps : (stream + 1) * taps, :] = short_rows[stream]
    gain_row = jnp.zeros((1, rows), jnp.float32)
    for group in range(groups):
        part = gain_line[:, group * rows : (group + 1) * rows]
        gain_row = gain_row + jnp.where(me == group, part, 0.0)
    coef_rows[3 * taps : 3 * taps + 1, :] = gain_row
    coef_cols[...] = coef_rows[...].T
    loads[2].wait()

    group_rows = 64
    scale = 1.0 / length

    def tokens_of(kind, picked):
        return jnp.concatenate([arrived[group, kind, picked, :] for group in range(groups)], 1)

    def finish(kind, picked, values):
        for group in range(groups):
            results[group, kind, picked, :] = values[:, group * span : (group + 1) * span].astype(
                jnp.bfloat16
            )

    def column(index, picked):
        return coef_cols[picked, index : index + 1]

    def delayed(values, offset):
        if offset == 0:
            return values
        lane = lax.broadcasted_iota(jnp.int32, values.shape, 1)
        return jnp.where(lane >= offset, pltpu.roll(values, offset, 1), 0.0)

    def advanced(values, offset):
        if offset == 0:
            return values
        lane = lax.broadcasted_iota(jnp.int32, values.shape, 1)
        moved = pltpu.roll(values, length - offset, 1)
        return jnp.where(lane < length - offset, moved, 0.0)

    for chunk in range(chunks):
        base = chunk * chunk_rows
        for kind in range(3):
            own_copies[chunk * 3 + kind].wait()
        for offset in range(1, groups):
            source = lax.rem(me + groups - offset, groups)
            for kind, pair in enumerate(in_pairs(me, source, chunk)):
                remote(
                    pair, in_send.at[chunk, kind, offset], in_recv.at[chunk, kind, offset], source
                ).wait_recv()

        @pl.loop(0, chunk_rows // group_rows)
        def _(step):
            inner = pl.ds(pl.multiple_of(step * group_rows, group_rows), group_rows)
            picked = pl.ds(pl.multiple_of(base + step * group_rows, group_rows), group_rows)
            primed = []
            for stream in range(3):
                wide = tokens_of(stream, picked).astype(jnp.float32)
                running = column(stream * taps, picked) * wide
                for offset in range(1, taps):
                    running = running + column(stream * taps + offset, picked) * delayed(
                        wide, offset
                    )
                primed.append(running)
                primed_buf[stream, inner, :] = running
            stacked[0, inner, :] = (primed[1] * primed[2]).astype(jnp.bfloat16)
            cot_wide = tokens_of(3, picked).astype(jnp.float32)
            stacked[1, inner, :] = (cot_wide * primed[0]).astype(jnp.bfloat16)
            stacked[2, inner, :] = tokens_of(4, picked)

        tile = 512

        @pl.loop(0, 2 * length // tile)
        def _(step):
            columns = pl.ds(pl.multiple_of(step * tile, tile), tile)
            left = stacked[...].reshape(3 * chunk_rows, length)
            total = jnp.dot(left, table[0, :, columns], preferred_element_type=jnp.float32)
            total += jnp.dot(left, table[1, :, columns], preferred_element_type=jnp.float32)
            freq[:, :, columns] = total.reshape(3, chunk_rows, tile)

        @pl.loop(0, chunk_rows // group_rows)
        def _(step):
            inner = pl.ds(pl.multiple_of(step * group_rows, group_rows), group_rows)
            first = lax.broadcasted_iota(jnp.int32, (group_rows, length), 1) == 0
            weight = jnp.where(first, 0.5 * scale, scale)
            mix_c, mix_s = freq[0, inner, :length], freq[0, inner, length:]
            grad_c, grad_s = freq[1, inner, :length], freq[1, inner, length:]
            kern_c, kern_s = freq[2, inner, :length], freq[2, inner, length:]

            def put(slot, left_c, left_s, right_c, right_s, sign):
                both = left_s * right_s
                even = left_c * right_c + sign * jnp.where(first, 0.0, both)
                odd = jnp.where(first, both, left_s * right_c - sign * (left_c * right_s))
                for half, part in enumerate((even, odd)):
                    value = part * weight
                    high = value.astype(jnp.bfloat16)
                    low = (value - high.astype(jnp.float32)).astype(jnp.bfloat16)
                    back_high[slot, inner, half * length : (half + 1) * length] = high
                    back_low[slot, inner, half * length : (half + 1) * length] = low

            put(0, mix_c, mix_s, kern_c, kern_s, -1.0)
            put(1, grad_c, grad_s, kern_c, kern_s, 1.0)
            put(2, grad_c, grad_s, mix_c, mix_s, 1.0)

        @pl.loop(0, length // tile)
        def _(step):
            picked = pl.ds(pl.multiple_of(step * tile, tile), tile)
            high = back_high[...].reshape(3 * chunk_rows, 2 * length)
            low = back_low[...].reshape(3 * chunk_rows, 2 * length)
            turned = (((1,), (1,)), ((), ()))
            total = lax.dot_general(
                high, table[0, picked, :], turned, preferred_element_type=jnp.float32
            )
            total += lax.dot_general(
                low, table[0, picked, :], turned, preferred_element_type=jnp.float32
            )
            total += lax.dot_general(
                high, table[1, picked, :], turned, preferred_element_type=jnp.float32
            )
            back_time[:, :, picked] = total.reshape(3, chunk_rows, tile)

        @pl.loop(0, chunk_rows // group_rows)
        def _(step):
            inner = pl.ds(pl.multiple_of(step * group_rows, group_rows), group_rows)
            picked = pl.ds(pl.multiple_of(base + step * group_rows, group_rows), group_rows)
            mixed = stacked[0, inner, :].astype(jnp.float32)
            gated = stacked[1, inner, :].astype(jnp.float32)
            gain = column(3 * taps, picked)
            long_wide = (
                (back_time[0, inner, :] + gain * mixed).astype(jnp.bfloat16).astype(jnp.float32)
            )
            mixed_back = (
                (back_time[1, inner, :] + gain * gated).astype(jnp.bfloat16).astype(jnp.float32)
            )
            finish(4, picked, back_time[2, inner, :])
            finish(0, picked, primed_buf[0, inner, :] * long_wide)
            cot_wide = tokens_of(3, picked).astype(jnp.float32)
            primed_grad = [
                cot_wide * long_wide,
                mixed_back * primed_buf[2, inner, :],
                mixed_back * primed_buf[1, inner, :],
            ]
            lane = lax.broadcasted_iota(jnp.int32, (group_rows, sums.shape[1]), 1)
            line = jnp.zeros((group_rows, sums.shape[1]), jnp.float32)
            for stream in range(3):
                moving = primed_grad[stream]
                wide = tokens_of(stream, picked).astype(jnp.float32)
                running = column(stream * taps, picked) * moving
                for offset in range(taps):
                    if offset:
                        running = running + column(stream * taps + offset, picked) * advanced(
                            moving, offset
                        )
                    total = jnp.sum(moving * delayed(wide, offset), axis=1, keepdims=True)
                    line = jnp.where(lane == stream * taps + offset, total, line)
                finish(1 + stream, picked, running)
            total = jnp.sum(gated * mixed, axis=1, keepdims=True)
            sums[picked, :] = jnp.where(lane == 3 * taps, total, line)

        for offset in range(1, groups):
            peer = lax.rem(me + offset, groups)
            for kind, pair in enumerate(out_pairs(peer, me, chunk)):
                copy = remote(
                    pair, out_send.at[chunk, kind, offset], out_recv.at[chunk, kind, offset], peer
                )
                copy.start()
                sent.append(copy)
        for kind, pair in enumerate(out_pairs(me, me, chunk)):
            copy = pltpu.make_async_copy(pair[0], pair[1], own_out.at[chunk, kind])
            copy.start()
            own_copies.append(copy)

    turned_sums = sums[...].T
    for stream in range(3):
        taps_out[stream] = turned_sums[stream * taps : (stream + 1) * taps, :]
    skip_out[...] = turned_sums[3 * taps : 3 * taps + 1, :]

    def small_pairs(owner):
        return [
            (taps_out, taps_hbm.at[:, :, at(owner, rows)]),
            (skip_out, skip_hbm.at[:, at(owner, rows)]),
        ]

    for kind, pair in enumerate(small_pairs(me)):
        copy = pltpu.make_async_copy(pair[0], pair[1], small_own.at[kind])
        copy.start()
        own_copies.append(copy)
        for offset in range(1, groups):
            peer = lax.rem(me + offset, groups)
            copy = remote(pair, small_send.at[kind, offset], small_recv.at[kind, offset], peer)
            copy.start()
            sent.append(copy)
    for copy in sent:
        copy.wait_send()
    for copy in own_copies[3 * chunks :]:
        copy.wait()
    for offset in range(1, groups):
        source = lax.rem(me + groups - offset, groups)
        for chunk in range(chunks):
            for kind, pair in enumerate(out_pairs(me, source, chunk)):
                remote(
                    pair, out_send.at[chunk, kind, offset], out_recv.at[chunk, kind, offset], source
                ).wait_recv()
        for kind, pair in enumerate(small_pairs(source)):
            remote(
                pair, small_send.at[kind, offset], small_recv.at[kind, offset], source
            ).wait_recv()


def settle_kernel(*refs):
    count = len(refs) // 2
    finished = refs[2 * count]
    copies = []
    for index in range(count):
        copy = pltpu.make_async_copy(refs[index], refs[count + index], finished.at[index])
        copy.start()
        copies.append(copy)
    for copy in copies:
        copy.wait()


def settle(values):
    return pl.pallas_call(
        settle_kernel,
        out_shape=tuple(jax.ShapeDtypeStruct(value.shape, value.dtype) for value in values),
        in_specs=[pl.BlockSpec(memory_space=pltpu.VMEM)] * len(values),
        out_specs=(pl.BlockSpec(memory_space=pltpu.HBM),) * len(values),
        scratch_shapes=[pltpu.SemaphoreType.DMA((len(values),))],
    )(*values)


def fused(features, cotangent, long_filter, short_filters, skip_gain, groups, chunks):
    channels, span = cotangent.shape
    rows = channels // groups
    length = span * groups
    taps = short_filters.shape[2]
    chunk_rows = rows // chunks
    hbm = pl.BlockSpec(memory_space=pltpu.HBM)
    dma = pltpu.SemaphoreType.DMA
    narrow = jnp.bfloat16
    outputs = pl.pallas_call(
        functools.partial(fused_kernel, (groups, rows, span, length, taps, chunks)),
        out_shape=(
            jax.ShapeDtypeStruct((channels, span), narrow),
            jax.ShapeDtypeStruct((3, channels, span), narrow),
            jax.ShapeDtypeStruct((channels, span), narrow),
            jax.ShapeDtypeStruct((3, taps, channels), jnp.float32),
            jax.ShapeDtypeStruct((1, channels), jnp.float32),
        ),
        in_specs=[hbm] * 6,
        out_specs=(pl.BlockSpec(memory_space=pltpu.VMEM),) * 5,
        scratch_shapes=[
            pltpu.VMEM((2, length, 2 * length), narrow),
            pltpu.VMEM((3, taps, rows), jnp.float32),
            pltpu.VMEM((1, channels), jnp.float32),
            pltpu.VMEM((rows, rows), jnp.float32),
            pltpu.VMEM((rows, rows), jnp.float32),
            pltpu.VMEM((groups, 5, rows, span), narrow),
            pltpu.VMEM((3, chunk_rows, length), narrow),
            pltpu.VMEM((3, chunk_rows, length), jnp.float32),
            pltpu.VMEM((3, chunk_rows, 2 * length), jnp.float32),
            pltpu.VMEM((3, chunk_rows, 2 * length), narrow),
            pltpu.VMEM((3, chunk_rows, 2 * length), narrow),
            pltpu.VMEM((3, chunk_rows, length), jnp.float32),
            pltpu.VMEM((groups, 5, rows, span), narrow),
            pltpu.VMEM((rows, rows), jnp.float32),
            pltpu.VMEM((3, taps, rows), jnp.float32),
            pltpu.VMEM((1, rows), jnp.float32),
            dma((3,)),
            dma((chunks, 3)),
            dma((chunks, 3)),
            dma((chunks, 3, groups)),
            dma((chunks, 3, groups)),
            dma((chunks, 3, groups)),
            dma((chunks, 3, groups)),
            dma((2,)),
            dma((2, groups)),
            dma((2, groups)),
        ],
        compiler_params=pltpu.CompilerParams(
            collective_id=0, has_side_effects=True
        ),
    )(
        features,
        cotangent,
        long_filter,
        jnp.swapaxes(short_filters, 1, 2),
        skip_gain[None],
        packed_tables(length),
    )
    gated_out, feature_grad, long_grad, taps_grad, gain_grad = settle(outputs)
    return gated_out, feature_grad, long_grad, jnp.swapaxes(taps_grad, 1, 2), gain_grad[0]


def dense_fits(features, short_filters, groups):
    channels, span = features.shape[1:]
    rows, length = channels // groups, span * groups
    return (
        channels % groups == 0
        and rows % 128 == 0
        and span % 128 == 0
        and length % 512 == 0
        and length <= 1024
        and rows <= 256
        and 3 * short_filters.shape[2] < 16
    )


def shards(features, cotangent, long_filter, short_filters, skip_gain):
    groups = lax.axis_size("seq")
    if dense_fits(features, short_filters, groups):
        return fused(
            features, cotangent, long_filter, short_filters, skip_gain, groups, chunk_count
        )
    seq_index = lax.axis_index("seq")
    channels = features.shape[1]
    per_group = channels // groups
    margin = short_filters.shape[2] - 1
    local_gain = lax.dynamic_slice_in_dim(skip_gain, seq_index * per_group, per_group, 0)
    stacked = jnp.concatenate([features, cotangent[None], long_filter[None]], 0)
    columns = lax.all_to_all(stacked, "seq", split_axis=1, concat_axis=2, tiled=True)
    weights = lax.dynamic_slice_in_dim(short_filters, seq_index * per_group, per_group, 1)
    length = columns.shape[2]
    history = jnp.pad(columns[:3].astype(jnp.float32), ((0, 0), (0, 0), (margin, 0)))
    primed = featurize(history, weights, margin, length)
    mixed_term = (primed[1] * primed[2]).astype(jnp.bfloat16)
    cot_wide = columns[3].astype(jnp.float32)
    gated_grad = (cot_wide * primed[0]).astype(jnp.bfloat16)
    long_out, mixed_grad, kernel_grad = spectral(mixed_term, gated_grad, columns[4], local_gain)
    long_wide = long_out.astype(jnp.float32)
    mixed_back = mixed_grad.astype(jnp.float32)
    gated_out = (primed[0] * long_wide).astype(jnp.bfloat16)
    primed_grad = jnp.stack([cot_wide * long_wide, mixed_back * primed[2], mixed_back * primed[1]])
    padded_grad = jnp.pad(primed_grad, ((0, 0), (0, 0), (0, margin)))
    feature_grad = unfeaturize(padded_grad, weights, length).astype(jnp.bfloat16)
    taps_grad = tap_grads(primed_grad, history, margin, length)
    gain_grad = jnp.sum(gated_grad.astype(jnp.float32) * mixed_term.astype(jnp.float32), axis=-1)
    results = jnp.concatenate([gated_out[None], feature_grad, kernel_grad[None]], 0)
    row_blocks = lax.all_to_all(results, "seq", split_axis=2, concat_axis=1, tiled=True)
    short_grad, skip_grad = (
        lax.all_gather(taps_grad, "seq", axis=1, tiled=True),
        lax.all_gather(gain_grad, "seq", axis=0, tiled=True),
    )
    return (row_blocks[0], row_blocks[1:4], row_blocks[4], short_grad, skip_grad)


def solution(mesh):
    placed = (
        P(None, "chan", "seq"),
        P("chan", "seq"),
        P("chan", "seq"),
        P(None, "chan", None),
        P("chan"),
    )
    return jax.shard_map(
        shards,
        mesh=mesh,
        in_specs=placed,
        out_specs=(
            P("chan", "seq"),
            P(None, "chan", "seq"),
            P("chan", "seq"),
            P(None, "chan", None),
            P("chan"),
        ),
        check_vma=False,
    )
```

```python
import functools
import math

import jax
import jax.numpy as jnp
import numpy as np
from jax import lax
from jax.experimental import pallas as pl
from jax.experimental.pallas import tpu as pltpu
from jax.sharding import PartitionSpec as P

inner_length = 128
radix_width = 8
chunk_count = 2


def phase_tables(row_count, col_count, length, direction):
    phase_index = (
        lax.iota(jnp.int32, row_count)[:, None] * lax.iota(jnp.int32, col_count)[None, :] % length
    )
    angles = direction * 2.0 * math.pi / length * phase_index.astype(jnp.float32)
    return (jnp.cos(angles), jnp.sin(angles))


def last_axis(operand, matrix):
    return jnp.einsum("...n,nk->...k", operand, matrix, precision=lax.Precision.HIGH)


def first_axis(operand, matrix):
    return jnp.einsum("...ab,ak->...kb", operand, matrix, precision=lax.Precision.HIGH)


def transform(real_part, imag_part, direction):
    length = real_part.shape[-1]
    if length <= inner_length or length % radix_width != 0:
        cos_table, sin_table = phase_tables(length, length, length, direction)
        return (
            last_axis(real_part, cos_table) - last_axis(imag_part, sin_table),
            last_axis(real_part, sin_table) + last_axis(imag_part, cos_table),
        )
    rest_length = length // radix_width
    grid_shape = real_part.shape[:-1] + (radix_width, rest_length)
    real_grid = real_part.reshape(grid_shape)
    imag_grid = imag_part.reshape(grid_shape)
    cos_table, sin_table = phase_tables(radix_width, radix_width, radix_width, direction)
    section_real = first_axis(real_grid, cos_table) - first_axis(imag_grid, sin_table)
    section_imag = first_axis(real_grid, sin_table) + first_axis(imag_grid, cos_table)
    twist_cos, twist_sin = phase_tables(radix_width, rest_length, length, direction)
    turned_real = section_real * twist_cos - section_imag * twist_sin
    turned_imag = section_real * twist_sin + section_imag * twist_cos
    inner_real, inner_imag = transform(turned_real, turned_imag, direction)
    return (
        jnp.swapaxes(inner_real, -1, -2).reshape(real_part.shape),
        jnp.swapaxes(inner_imag, -1, -2).reshape(real_part.shape),
    )


def spectral(mixed_term, gated_grad, kernel, local_gain):
    length = mixed_term.shape[-1]
    mixed_wide = mixed_term.astype(jnp.float32)
    gated_wide = gated_grad.astype(jnp.float32)
    kernel_wide = kernel.astype(jnp.float32)
    extend = ((0, 0), (0, length))
    real_in = jnp.stack([jnp.pad(mixed_wide, extend), jnp.pad(kernel_wide, extend)])
    imag_in = jnp.stack(
        [jnp.pad(gated_wide, extend), jnp.zeros((kernel_wide.shape[0], 2 * length), jnp.float32)]
    )
    freq_real, freq_imag = transform(real_in, imag_in, -1.0)
    packed_real = freq_real[0]
    packed_imag = freq_imag[0]
    mirror_real = jnp.roll(jnp.flip(packed_real, -1), 1, -1)
    mirror_imag = jnp.roll(jnp.flip(packed_imag, -1), 1, -1)
    mix_real = 0.5 * (packed_real + mirror_real)
    mix_imag = 0.5 * (packed_imag - mirror_imag)
    grad_real = 0.5 * (packed_imag + mirror_imag)
    grad_imag = 0.5 * (mirror_real - packed_real)
    kern_real = freq_real[1]
    kern_imag = freq_imag[1]
    conv_real = mix_real * kern_real - mix_imag * kern_imag
    conv_imag = mix_real * kern_imag + mix_imag * kern_real
    corr_real = grad_real * kern_real + grad_imag * kern_imag
    corr_imag = grad_imag * kern_real - grad_real * kern_imag
    cross_real = grad_real * mix_real + grad_imag * mix_imag
    cross_imag = grad_imag * mix_real - grad_real * mix_imag
    back_real = jnp.stack([conv_real - corr_imag, cross_real])
    back_imag = jnp.stack([conv_imag + corr_real, cross_imag])
    time_real, time_imag = transform(back_real, back_imag, 1.0)
    inverse_scale = 1.0 / (2 * length)
    conv_part = time_real[0, :, :length] * inverse_scale
    corr_part = time_imag[0, :, :length] * inverse_scale
    cross_part = time_real[1, :, :length] * inverse_scale
    gain_column = local_gain[:, None]
    long_out = (conv_part + gain_column * mixed_wide).astype(jnp.bfloat16)
    mixed_grad = (corr_part + gain_column * gated_wide).astype(jnp.bfloat16)
    return (long_out, mixed_grad, cross_part.astype(jnp.bfloat16))


def featurize(history, weights, margin, span_count):
    running = weights[:, :, 0:1] * history[:, :, margin : margin + span_count]
    for offset in range(1, margin + 1):
        running = (
            running
            + weights[:, :, offset : offset + 1]
            * history[:, :, margin - offset : margin - offset + span_count]
        )
    return running


def unfeaturize(padded_grad, weights, span_count):
    running = weights[:, :, 0:1] * padded_grad[:, :, 0:span_count]
    for offset in range(1, weights.shape[2]):
        running = (
            running
            + weights[:, :, offset : offset + 1] * padded_grad[:, :, offset : offset + span_count]
        )
    return running


def tap_grads(primed_grad, history, margin, span_count):
    columns = []
    for offset in range(margin + 1):
        columns.append(
            jnp.sum(
                primed_grad * history[:, :, margin - offset : margin - offset + span_count], axis=-1
            )
        )
    return jnp.stack(columns, axis=-1)


def packed_tables(length):
    steps = np.arange(length)
    phase = (steps[:, None] * steps[None, :]) % (2 * length)
    angles = np.pi / length * phase
    sines = np.sin(angles)
    sines[:, 0] = 1.0 - 2.0 * (steps % 2)
    table = np.concatenate([np.cos(angles), sines], 1).astype(np.float32)
    high = table.astype(jnp.bfloat16)
    low = (table - high.astype(np.float32)).astype(jnp.bfloat16)
    return np.stack([high, low])


def fused_kernel(
    sizes,
    feat_hbm,
    cot_hbm,
    filt_hbm,
    short_hbm,
    gain_hbm,
    table_hbm,
    gated_hbm,
    grad_hbm,
    long_hbm,
    taps_hbm,
    skip_hbm,
    table,
    short_rows,
    gain_line,
    coef_rows,
    coef_cols,
    arrived,
    stacked,
    primed_buf,
    freq,
    back_both,
    back_time,
    results,
    sums,
    taps_out,
    skip_out,
    load_sem,
    own_in,
    own_out,
    in_send,
    in_recv,
    out_send,
    out_recv,
    small_own,
    small_send,
    small_recv,
):
    groups, rows, span, length, taps, chunks = sizes
    chunk_rows = rows // chunks
    me = lax.axis_index("seq")

    def at(index, extent):
        return pl.ds(pl.multiple_of(index * extent, extent), extent)

    def chan_rows(owner, chunk):
        start = owner * rows + chunk * chunk_rows
        return pl.ds(pl.multiple_of(start, chunk_rows), chunk_rows)

    barrier = pltpu.get_barrier_semaphore()
    for offset in range(1, groups):
        pl.semaphore_signal(
            barrier,
            inc=1,
            device_id={"seq": lax.rem(me + offset, groups)},
            device_id_type=pl.DeviceIdType.MESH,
        )
    loads = [
        pltpu.make_async_copy(short_hbm.at[:, :, at(me, rows)], short_rows, load_sem.at[0]),
        pltpu.make_async_copy(gain_hbm, gain_line, load_sem.at[1]),
        pltpu.make_async_copy(table_hbm, table, load_sem.at[2]),
    ]
    for load in loads:
        load.start()

    def in_pairs(owner, source, chunk):
        taken = chan_rows(owner, chunk)
        kept = pl.ds(chunk * chunk_rows, chunk_rows)
        return [
            (filt_hbm.at[taken, :], arrived.at[source, 4, kept, :]),
            (feat_hbm.at[:, taken, :], arrived.at[source, 0:3, kept, :]),
            (cot_hbm.at[taken, :], arrived.at[source, 3, kept, :]),
        ]

    def out_pairs(target, owner, chunk):
        kept = pl.ds(chunk * chunk_rows, chunk_rows)
        placed = chan_rows(owner, chunk)
        return [
            (results.at[target, 0, kept, :], gated_hbm.at[placed, :]),
            (results.at[target, 1:4, kept, :], grad_hbm.at[:, placed, :]),
            (results.at[target, 4, kept, :], long_hbm.at[placed, :]),
        ]

    def remote(pair, send_sem, recv_sem, peer):
        return pltpu.make_async_remote_copy(
            src_ref=pair[0],
            dst_ref=pair[1],
            send_sem=send_sem,
            recv_sem=recv_sem,
            device_id={"seq": peer},
            device_id_type=pl.DeviceIdType.MESH,
        )

    own_copies = []
    for chunk in range(chunks):
        for kind, pair in enumerate(in_pairs(me, me, chunk)):
            copy = pltpu.make_async_copy(pair[0], pair[1], own_in.at[chunk, kind])
            copy.start()
            own_copies.append(copy)

    pl.semaphore_wait(barrier, groups - 1)

    sent = []
    for chunk in range(chunks):
        for offset in range(1, groups):
            peer = lax.rem(me + offset, groups)
            for kind, pair in enumerate(in_pairs(peer, me, chunk)):
                copy = remote(
                    pair, in_send.at[chunk, kind, offset], in_recv.at[chunk, kind, offset], peer
                )
                copy.start()
                sent.append(copy)

    loads[0].wait()
    loads[1].wait()
    coef_rows[...] = jnp.zeros_like(coef_rows)
    for stream in range(3):
        coef_rows[stream * taps : (stream + 1) * taps, :] = short_rows[stream]
    gain_row = jnp.zeros((1, rows), jnp.float32)
    for group in range(groups):
        part = gain_line[:, group * rows : (group + 1) * rows]
        gain_row = gain_row + jnp.where(me == group, part, 0.0)
    coef_rows[3 * taps : 3 * taps + 1, :] = gain_row
    coef_cols[...] = coef_rows[...].T
    loads[2].wait()

    group_rows = 64
    scale = 1.0 / length

    def tokens_of(kind, picked):
        return jnp.concatenate([arrived[group, kind, picked, :] for group in range(groups)], 1)

    def finish(kind, picked, values):
        for group in range(groups):
            results[group, kind, picked, :] = values[:, group * span : (group + 1) * span].astype(
                jnp.bfloat16
            )

    def column(index, picked):
        return coef_cols[picked, index : index + 1]

    def delayed(values, offset):
        if offset == 0:
            return values
        lane = lax.broadcasted_iota(jnp.int32, values.shape, 1)
        return jnp.where(lane >= offset, pltpu.roll(values, offset, 1), 0.0)

    def advanced(values, offset):
        if offset == 0:
            return values
        lane = lax.broadcasted_iota(jnp.int32, values.shape, 1)
        moved = pltpu.roll(values, length - offset, 1)
        return jnp.where(lane < length - offset, moved, 0.0)

    def send_kinds(chunk, kinds):
        for offset in range(1, groups):
            peer = lax.rem(me + offset, groups)
            pairs = out_pairs(peer, me, chunk)
            for kind in kinds:
                copy = remote(
                    pairs[kind],
                    out_send.at[chunk, kind, offset],
                    out_recv.at[chunk, kind, offset],
                    peer,
                )
                copy.start()
                sent.append(copy)

    for chunk in range(chunks):
        base = chunk * chunk_rows
        for kind in range(3):
            own_copies[chunk * 3 + kind].wait()
        for offset in range(1, groups):
            source = lax.rem(me + groups - offset, groups)
            for kind, pair in enumerate(in_pairs(me, source, chunk)):
                remote(
                    pair, in_send.at[chunk, kind, offset], in_recv.at[chunk, kind, offset], source
                ).wait_recv()

        @pl.loop(0, chunk_rows // group_rows)
        def _(step):
            inner = pl.ds(pl.multiple_of(step * group_rows, group_rows), group_rows)
            picked = pl.ds(pl.multiple_of(base + step * group_rows, group_rows), group_rows)
            primed = []
            for stream in range(3):
                wide = tokens_of(stream, picked).astype(jnp.float32)
                running = column(stream * taps, picked) * wide
                for offset in range(1, taps):
                    running = running + column(stream * taps + offset, picked) * delayed(
                        wide, offset
                    )
                primed.append(running)
                primed_buf[stream, inner, :] = running
            stacked[0, inner, :] = (primed[1] * primed[2]).astype(jnp.bfloat16)
            cot_wide = tokens_of(3, picked).astype(jnp.float32)
            stacked[1, inner, :] = (cot_wide * primed[0]).astype(jnp.bfloat16)
            stacked[2, inner, :] = tokens_of(4, picked)

        tile = 512

        @pl.loop(0, 2 * length // tile)
        def _(step):
            columns = pl.ds(pl.multiple_of(step * tile, tile), tile)
            left = stacked[...].reshape(3 * chunk_rows, length)
            total = jnp.dot(left, table[0, :, columns], preferred_element_type=jnp.float32)
            total += jnp.dot(left, table[1, :, columns], preferred_element_type=jnp.float32)
            freq[:, :, columns] = total.reshape(3, chunk_rows, tile)

        @pl.loop(0, chunk_rows // group_rows)
        def _(step):
            inner = pl.ds(pl.multiple_of(step * group_rows, group_rows), group_rows)
            first = lax.broadcasted_iota(jnp.int32, (group_rows, length), 1) == 0
            weight = jnp.where(first, 0.5 * scale, scale)
            mix_c, mix_s = freq[0, inner, :length], freq[0, inner, length:]
            grad_c, grad_s = freq[1, inner, :length], freq[1, inner, length:]
            kern_c, kern_s = freq[2, inner, :length], freq[2, inner, length:]

            def put(slot, left_c, left_s, right_c, right_s, sign):
                both = left_s * right_s
                even = left_c * right_c + sign * jnp.where(first, 0.0, both)
                odd = jnp.where(first, both, left_s * right_c - sign * (left_c * right_s))
                for half, part in enumerate((even, odd)):
                    value = part * weight
                    high = value.astype(jnp.bfloat16)
                    low = (value - high.astype(jnp.float32)).astype(jnp.bfloat16)
                    back_both[slot, inner, half * length : (half + 1) * length] = high
                    back_both[3 + slot, inner, half * length : (half + 1) * length] = low

            put(0, mix_c, mix_s, kern_c, kern_s, -1.0)
            put(1, grad_c, grad_s, kern_c, kern_s, 1.0)
            put(2, grad_c, grad_s, mix_c, mix_s, 1.0)

        @pl.loop(0, length // tile)
        def _(step):
            picked = pl.ds(pl.multiple_of(step * tile, tile), tile)
            both = back_both[...].reshape(6 * chunk_rows, 2 * length)
            high = both[: 3 * chunk_rows]
            turned = (((1,), (1,)), ((), ()))
            pair = lax.dot_general(
                both, table[0, picked, :], turned, preferred_element_type=jnp.float32
            )
            total = pair[: 3 * chunk_rows] + pair[3 * chunk_rows :]
            total += lax.dot_general(
                high, table[1, picked, :], turned, preferred_element_type=jnp.float32
            )
            back_time[:, :, picked] = total.reshape(3, chunk_rows, tile)

        finish(4, pl.ds(base, chunk_rows), back_time[2])
        send_kinds(chunk, (2,))

        @pl.loop(0, chunk_rows // group_rows)
        def _(step):
            inner = pl.ds(pl.multiple_of(step * group_rows, group_rows), group_rows)
            picked = pl.ds(pl.multiple_of(base + step * group_rows, group_rows), group_rows)
            mixed = stacked[0, inner, :].astype(jnp.float32)
            gated = stacked[1, inner, :].astype(jnp.float32)
            gain = column(3 * taps, picked)
            long_wide = (
                (back_time[0, inner, :] + gain * mixed).astype(jnp.bfloat16).astype(jnp.float32)
            )
            mixed_back = (
                (back_time[1, inner, :] + gain * gated).astype(jnp.bfloat16).astype(jnp.float32)
            )
            finish(0, picked, primed_buf[0, inner, :] * long_wide)
            cot_wide = tokens_of(3, picked).astype(jnp.float32)
            primed_grad = [
                cot_wide * long_wide,
                mixed_back * primed_buf[2, inner, :],
                mixed_back * primed_buf[1, inner, :],
            ]
            lane = lax.broadcasted_iota(jnp.int32, (group_rows, sums.shape[1]), 1)
            line = jnp.zeros((group_rows, sums.shape[1]), jnp.float32)
            for stream in range(3):
                moving = primed_grad[stream]
                wide = tokens_of(stream, picked).astype(jnp.float32)
                running = column(stream * taps, picked) * moving
                for offset in range(taps):
                    if offset:
                        running = running + column(stream * taps + offset, picked) * advanced(
                            moving, offset
                        )
                    total = jnp.sum(moving * delayed(wide, offset), axis=1, keepdims=True)
                    line = jnp.where(lane == stream * taps + offset, total, line)
                finish(1 + stream, picked, running)
            total = jnp.sum(gated * mixed, axis=1, keepdims=True)
            sums[picked, :] = jnp.where(lane == 3 * taps, total, line)

        send_kinds(chunk, (0, 1))
        for kind, pair in enumerate(out_pairs(me, me, chunk)):
            copy = pltpu.make_async_copy(pair[0], pair[1], own_out.at[chunk, kind])
            copy.start()
            own_copies.append(copy)

    turned_sums = sums[...].T
    for stream in range(3):
        taps_out[stream] = turned_sums[stream * taps : (stream + 1) * taps, :]
    skip_out[...] = turned_sums[3 * taps : 3 * taps + 1, :]

    def small_pairs(owner):
        return [
            (taps_out, taps_hbm.at[:, :, at(owner, rows)]),
            (skip_out, skip_hbm.at[:, at(owner, rows)]),
        ]

    for kind, pair in enumerate(small_pairs(me)):
        copy = pltpu.make_async_copy(pair[0], pair[1], small_own.at[kind])
        copy.start()
        own_copies.append(copy)
        for offset in range(1, groups):
            peer = lax.rem(me + offset, groups)
            copy = remote(pair, small_send.at[kind, offset], small_recv.at[kind, offset], peer)
            copy.start()
            sent.append(copy)
    for copy in sent:
        copy.wait_send()
    for copy in own_copies[3 * chunks :]:
        copy.wait()
    for offset in range(1, groups):
        source = lax.rem(me + groups - offset, groups)
        for chunk in range(chunks):
            for kind, pair in enumerate(out_pairs(me, source, chunk)):
                remote(
                    pair, out_send.at[chunk, kind, offset], out_recv.at[chunk, kind, offset], source
                ).wait_recv()
        for kind, pair in enumerate(small_pairs(source)):
            remote(
                pair, small_send.at[kind, offset], small_recv.at[kind, offset], source
            ).wait_recv()


def settle_kernel(*refs):
    count = len(refs) // 2
    finished = refs[2 * count]
    copies = []
    for index in range(count):
        copy = pltpu.make_async_copy(refs[index], refs[count + index], finished.at[index])
        copy.start()
        copies.append(copy)
    for copy in copies:
        copy.wait()


def settle(values):
    return pl.pallas_call(
        settle_kernel,
        out_shape=tuple(jax.ShapeDtypeStruct(value.shape, value.dtype) for value in values),
        in_specs=[pl.BlockSpec(memory_space=pltpu.VMEM)] * len(values),
        out_specs=(pl.BlockSpec(memory_space=pltpu.HBM),) * len(values),
        scratch_shapes=[pltpu.SemaphoreType.DMA((len(values),))],
    )(*values)


def fused(features, cotangent, long_filter, short_filters, skip_gain, groups, chunks):
    channels, span = cotangent.shape
    rows = channels // groups
    length = span * groups
    taps = short_filters.shape[2]
    chunk_rows = rows // chunks
    hbm = pl.BlockSpec(memory_space=pltpu.HBM)
    dma = pltpu.SemaphoreType.DMA
    narrow = jnp.bfloat16
    outputs = pl.pallas_call(
        functools.partial(fused_kernel, (groups, rows, span, length, taps, chunks)),
        out_shape=(
            jax.ShapeDtypeStruct((channels, span), narrow),
            jax.ShapeDtypeStruct((3, channels, span), narrow),
            jax.ShapeDtypeStruct((channels, span), narrow),
            jax.ShapeDtypeStruct((3, taps, channels), jnp.float32),
            jax.ShapeDtypeStruct((1, channels), jnp.float32),
        ),
        in_specs=[hbm] * 6,
        out_specs=(pl.BlockSpec(memory_space=pltpu.VMEM),) * 5,
        scratch_shapes=[
            pltpu.VMEM((2, length, 2 * length), narrow),
            pltpu.VMEM((3, taps, rows), jnp.float32),
            pltpu.VMEM((1, channels), jnp.float32),
            pltpu.VMEM((rows, rows), jnp.float32),
            pltpu.VMEM((rows, rows), jnp.float32),
            pltpu.VMEM((groups, 5, rows, span), narrow),
            pltpu.VMEM((3, chunk_rows, length), narrow),
            pltpu.VMEM((3, chunk_rows, length), jnp.float32),
            pltpu.VMEM((3, chunk_rows, 2 * length), jnp.float32),
            pltpu.VMEM((6, chunk_rows, 2 * length), narrow),
            pltpu.VMEM((3, chunk_rows, length), jnp.float32),
            pltpu.VMEM((groups, 5, rows, span), narrow),
            pltpu.VMEM((rows, rows), jnp.float32),
            pltpu.VMEM((3, taps, rows), jnp.float32),
            pltpu.VMEM((1, rows), jnp.float32),
            dma((3,)),
            dma((chunks, 3)),
            dma((chunks, 3)),
            dma((chunks, 3, groups)),
            dma((chunks, 3, groups)),
            dma((chunks, 3, groups)),
            dma((chunks, 3, groups)),
            dma((2,)),
            dma((2, groups)),
            dma((2, groups)),
        ],
        compiler_params=pltpu.CompilerParams(
            collective_id=0, has_side_effects=True
        ),
    )(
        features,
        cotangent,
        long_filter,
        jnp.swapaxes(short_filters, 1, 2),
        skip_gain[None],
        packed_tables(length),
    )
    gated_out, feature_grad, long_grad, taps_grad, gain_grad = settle(outputs)
    return gated_out, feature_grad, long_grad, jnp.swapaxes(taps_grad, 1, 2), gain_grad[0]


def dense_fits(features, short_filters, groups):
    channels, span = features.shape[1:]
    rows, length = channels // groups, span * groups
    return (
        channels % groups == 0
        and rows % 128 == 0
        and span % 128 == 0
        and length % 512 == 0
        and length <= 1024
        and rows <= 256
        and 3 * short_filters.shape[2] < 16
    )


def shards(features, cotangent, long_filter, short_filters, skip_gain):
    groups = lax.axis_size("seq")
    if dense_fits(features, short_filters, groups):
        return fused(
            features, cotangent, long_filter, short_filters, skip_gain, groups, chunk_count
        )
    seq_index = lax.axis_index("seq")
    channels = features.shape[1]
    per_group = channels // groups
    margin = short_filters.shape[2] - 1
    local_gain = lax.dynamic_slice_in_dim(skip_gain, seq_index * per_group, per_group, 0)
    stacked = jnp.concatenate([features, cotangent[None], long_filter[None]], 0)
    columns = lax.all_to_all(stacked, "seq", split_axis=1, concat_axis=2, tiled=True)
    weights = lax.dynamic_slice_in_dim(short_filters, seq_index * per_group, per_group, 1)
    length = columns.shape[2]
    history = jnp.pad(columns[:3].astype(jnp.float32), ((0, 0), (0, 0), (margin, 0)))
    primed = featurize(history, weights, margin, length)
    mixed_term = (primed[1] * primed[2]).astype(jnp.bfloat16)
    cot_wide = columns[3].astype(jnp.float32)
    gated_grad = (cot_wide * primed[0]).astype(jnp.bfloat16)
    long_out, mixed_grad, kernel_grad = spectral(mixed_term, gated_grad, columns[4], local_gain)
    long_wide = long_out.astype(jnp.float32)
    mixed_back = mixed_grad.astype(jnp.float32)
    gated_out = (primed[0] * long_wide).astype(jnp.bfloat16)
    primed_grad = jnp.stack([cot_wide * long_wide, mixed_back * primed[2], mixed_back * primed[1]])
    padded_grad = jnp.pad(primed_grad, ((0, 0), (0, 0), (0, margin)))
    feature_grad = unfeaturize(padded_grad, weights, length).astype(jnp.bfloat16)
    taps_grad = tap_grads(primed_grad, history, margin, length)
    gain_grad = jnp.sum(gated_grad.astype(jnp.float32) * mixed_term.astype(jnp.float32), axis=-1)
    results = jnp.concatenate([gated_out[None], feature_grad, kernel_grad[None]], 0)
    row_blocks = lax.all_to_all(results, "seq", split_axis=2, concat_axis=1, tiled=True)
    short_grad, skip_grad = (
        lax.all_gather(taps_grad, "seq", axis=1, tiled=True),
        lax.all_gather(gain_grad, "seq", axis=0, tiled=True),
    )
    return (row_blocks[0], row_blocks[1:4], row_blocks[4], short_grad, skip_grad)


def solution(mesh):
    placed = (
        P(None, "chan", "seq"),
        P("chan", "seq"),
        P("chan", "seq"),
        P(None, "chan", None),
        P("chan"),
    )
    return jax.shard_map(
        shards,
        mesh=mesh,
        in_specs=placed,
        out_specs=(
            P("chan", "seq"),
            P(None, "chan", "seq"),
            P("chan", "seq"),
            P(None, "chan", None),
            P("chan"),
        ),
        check_vma=False,
    )
```

```python
import functools
import math

import jax
import jax.numpy as jnp
import numpy as np
from jax import lax
from jax.experimental import pallas as pl
from jax.experimental.pallas import tpu as pltpu
from jax.sharding import PartitionSpec as P

inner_length = 128
radix_width = 8
chunk_count = 2


def phase_tables(row_count, col_count, length, direction):
    phase_index = (
        lax.iota(jnp.int32, row_count)[:, None] * lax.iota(jnp.int32, col_count)[None, :] % length
    )
    angles = direction * 2.0 * math.pi / length * phase_index.astype(jnp.float32)
    return (jnp.cos(angles), jnp.sin(angles))


def last_axis(operand, matrix):
    return jnp.einsum("...n,nk->...k", operand, matrix, precision=lax.Precision.HIGH)


def first_axis(operand, matrix):
    return jnp.einsum("...ab,ak->...kb", operand, matrix, precision=lax.Precision.HIGH)


def transform(real_part, imag_part, direction):
    length = real_part.shape[-1]
    if length <= inner_length or length % radix_width != 0:
        cos_table, sin_table = phase_tables(length, length, length, direction)
        return (
            last_axis(real_part, cos_table) - last_axis(imag_part, sin_table),
            last_axis(real_part, sin_table) + last_axis(imag_part, cos_table),
        )
    rest_length = length // radix_width
    grid_shape = real_part.shape[:-1] + (radix_width, rest_length)
    real_grid = real_part.reshape(grid_shape)
    imag_grid = imag_part.reshape(grid_shape)
    cos_table, sin_table = phase_tables(radix_width, radix_width, radix_width, direction)
    section_real = first_axis(real_grid, cos_table) - first_axis(imag_grid, sin_table)
    section_imag = first_axis(real_grid, sin_table) + first_axis(imag_grid, cos_table)
    twist_cos, twist_sin = phase_tables(radix_width, rest_length, length, direction)
    turned_real = section_real * twist_cos - section_imag * twist_sin
    turned_imag = section_real * twist_sin + section_imag * twist_cos
    inner_real, inner_imag = transform(turned_real, turned_imag, direction)
    return (
        jnp.swapaxes(inner_real, -1, -2).reshape(real_part.shape),
        jnp.swapaxes(inner_imag, -1, -2).reshape(real_part.shape),
    )


def spectral(mixed_term, gated_grad, kernel, local_gain):
    length = mixed_term.shape[-1]
    mixed_wide = mixed_term.astype(jnp.float32)
    gated_wide = gated_grad.astype(jnp.float32)
    kernel_wide = kernel.astype(jnp.float32)
    extend = ((0, 0), (0, length))
    real_in = jnp.stack([jnp.pad(mixed_wide, extend), jnp.pad(kernel_wide, extend)])
    imag_in = jnp.stack(
        [jnp.pad(gated_wide, extend), jnp.zeros((kernel_wide.shape[0], 2 * length), jnp.float32)]
    )
    freq_real, freq_imag = transform(real_in, imag_in, -1.0)
    packed_real = freq_real[0]
    packed_imag = freq_imag[0]
    mirror_real = jnp.roll(jnp.flip(packed_real, -1), 1, -1)
    mirror_imag = jnp.roll(jnp.flip(packed_imag, -1), 1, -1)
    mix_real = 0.5 * (packed_real + mirror_real)
    mix_imag = 0.5 * (packed_imag - mirror_imag)
    grad_real = 0.5 * (packed_imag + mirror_imag)
    grad_imag = 0.5 * (mirror_real - packed_real)
    kern_real = freq_real[1]
    kern_imag = freq_imag[1]
    conv_real = mix_real * kern_real - mix_imag * kern_imag
    conv_imag = mix_real * kern_imag + mix_imag * kern_real
    corr_real = grad_real * kern_real + grad_imag * kern_imag
    corr_imag = grad_imag * kern_real - grad_real * kern_imag
    cross_real = grad_real * mix_real + grad_imag * mix_imag
    cross_imag = grad_imag * mix_real - grad_real * mix_imag
    back_real = jnp.stack([conv_real - corr_imag, cross_real])
    back_imag = jnp.stack([conv_imag + corr_real, cross_imag])
    time_real, time_imag = transform(back_real, back_imag, 1.0)
    inverse_scale = 1.0 / (2 * length)
    conv_part = time_real[0, :, :length] * inverse_scale
    corr_part = time_imag[0, :, :length] * inverse_scale
    cross_part = time_real[1, :, :length] * inverse_scale
    gain_column = local_gain[:, None]
    long_out = (conv_part + gain_column * mixed_wide).astype(jnp.bfloat16)
    mixed_grad = (corr_part + gain_column * gated_wide).astype(jnp.bfloat16)
    return (long_out, mixed_grad, cross_part.astype(jnp.bfloat16))


def featurize(history, weights, margin, span_count):
    running = weights[:, :, 0:1] * history[:, :, margin : margin + span_count]
    for offset in range(1, margin + 1):
        running = (
            running
            + weights[:, :, offset : offset + 1]
            * history[:, :, margin - offset : margin - offset + span_count]
        )
    return running


def unfeaturize(padded_grad, weights, span_count):
    running = weights[:, :, 0:1] * padded_grad[:, :, 0:span_count]
    for offset in range(1, weights.shape[2]):
        running = (
            running
            + weights[:, :, offset : offset + 1] * padded_grad[:, :, offset : offset + span_count]
        )
    return running


def tap_grads(primed_grad, history, margin, span_count):
    columns = []
    for offset in range(margin + 1):
        columns.append(
            jnp.sum(
                primed_grad * history[:, :, margin - offset : margin - offset + span_count], axis=-1
            )
        )
    return jnp.stack(columns, axis=-1)


def packed_tables(length):
    steps = np.arange(length)
    phase = (steps[:, None] * steps[None, :]) % (2 * length)
    angles = np.pi / length * phase
    sines = np.sin(angles)
    sines[:, 0] = 1.0 - 2.0 * (steps % 2)
    table = np.concatenate([np.cos(angles), sines], 1).astype(np.float32)
    high = table.astype(jnp.bfloat16)
    low = (table - high.astype(np.float32)).astype(jnp.bfloat16)
    return np.stack([high, low])


def fused_kernel(
    sizes,
    feat_hbm,
    cot_hbm,
    filt_hbm,
    short_hbm,
    gain_hbm,
    table_hbm,
    gated_hbm,
    grad_hbm,
    long_hbm,
    taps_hbm,
    skip_hbm,
    table,
    short_rows,
    gain_line,
    coef_rows,
    coef_cols,
    arrived,
    stacked,
    primed_buf,
    freq,
    back_both,
    back_time,
    results,
    sums,
    taps_out,
    skip_out,
    load_sem,
    own_in,
    own_out,
    in_send,
    in_recv,
    out_send,
    out_recv,
    small_own,
    small_send,
    small_recv,
):
    groups, rows, span, length, taps, chunks = sizes
    chunk_rows = rows // chunks
    me = lax.axis_index("seq")

    def at(index, extent):
        return pl.ds(pl.multiple_of(index * extent, extent), extent)

    def chan_rows(owner, chunk):
        start = owner * rows + chunk * chunk_rows
        return pl.ds(pl.multiple_of(start, chunk_rows), chunk_rows)

    barrier = pltpu.get_barrier_semaphore()
    for offset in range(1, groups):
        pl.semaphore_signal(
            barrier,
            inc=1,
            device_id={"seq": lax.rem(me + offset, groups)},
            device_id_type=pl.DeviceIdType.MESH,
        )
    loads = [
        pltpu.make_async_copy(short_hbm.at[:, :, at(me, rows)], short_rows, load_sem.at[0]),
        pltpu.make_async_copy(gain_hbm, gain_line, load_sem.at[1]),
        pltpu.make_async_copy(table_hbm, table, load_sem.at[2]),
    ]
    for load in loads:
        load.start()

    def in_pairs(owner, source, chunk):
        taken = chan_rows(owner, chunk)
        kept = pl.ds(chunk * chunk_rows, chunk_rows)
        return [
            (filt_hbm.at[taken, :], arrived.at[source, 4, kept, :]),
            (feat_hbm.at[:, taken, :], arrived.at[source, 0:3, kept, :]),
            (cot_hbm.at[taken, :], arrived.at[source, 3, kept, :]),
        ]

    def out_pairs(target, owner, chunk):
        kept = pl.ds(chunk * chunk_rows, chunk_rows)
        placed = chan_rows(owner, chunk)
        return [
            (results.at[target, 0, kept, :], gated_hbm.at[placed, :]),
            (results.at[target, 1:4, kept, :], grad_hbm.at[:, placed, :]),
            (results.at[target, 4, kept, :], long_hbm.at[placed, :]),
        ]

    def remote(pair, send_sem, recv_sem, peer):
        return pltpu.make_async_remote_copy(
            src_ref=pair[0],
            dst_ref=pair[1],
            send_sem=send_sem,
            recv_sem=recv_sem,
            device_id={"seq": peer},
            device_id_type=pl.DeviceIdType.MESH,
        )

    own_copies = []
    for chunk in range(chunks):
        for kind, pair in enumerate(in_pairs(me, me, chunk)):
            copy = pltpu.make_async_copy(pair[0], pair[1], own_in.at[chunk, kind])
            copy.start()
            own_copies.append(copy)

    pl.semaphore_wait(barrier, groups - 1)

    sent = []
    for chunk in range(chunks):
        for offset in range(1, groups):
            peer = lax.rem(me + offset, groups)
            for kind, pair in enumerate(in_pairs(peer, me, chunk)):
                copy = remote(
                    pair, in_send.at[chunk, kind, offset], in_recv.at[chunk, kind, offset], peer
                )
                copy.start()
                sent.append(copy)

    loads[0].wait()
    loads[1].wait()
    coef_rows[...] = jnp.zeros_like(coef_rows)
    for stream in range(3):
        coef_rows[stream * taps : (stream + 1) * taps, :] = short_rows[stream]
    gain_row = jnp.zeros((1, rows), jnp.float32)
    for group in range(groups):
        part = gain_line[:, group * rows : (group + 1) * rows]
        gain_row = gain_row + jnp.where(me == group, part, 0.0)
    coef_rows[3 * taps : 3 * taps + 1, :] = gain_row
    coef_cols[...] = coef_rows[...].T
    loads[2].wait()

    group_rows = 64
    scale = 1.0 / length

    def tokens_of(kind, picked):
        return jnp.concatenate([arrived[group, kind, picked, :] for group in range(groups)], 1)

    def finish(kind, picked, values):
        for group in range(groups):
            results[group, kind, picked, :] = values[:, group * span : (group + 1) * span].astype(
                jnp.bfloat16
            )

    def column(index, picked):
        return coef_cols[picked, index : index + 1]

    def delayed(values, offset):
        if offset == 0:
            return values
        lane = lax.broadcasted_iota(jnp.int32, values.shape, 1)
        return jnp.where(lane >= offset, pltpu.roll(values, offset, 1), 0.0)

    def advanced(values, offset):
        if offset == 0:
            return values
        lane = lax.broadcasted_iota(jnp.int32, values.shape, 1)
        moved = pltpu.roll(values, length - offset, 1)
        return jnp.where(lane < length - offset, moved, 0.0)

    def send_kinds(chunk, kinds):
        for offset in range(1, groups):
            peer = lax.rem(me + offset, groups)
            pairs = out_pairs(peer, me, chunk)
            for kind in kinds:
                copy = remote(
                    pairs[kind],
                    out_send.at[chunk, kind, offset],
                    out_recv.at[chunk, kind, offset],
                    peer,
                )
                copy.start()
                sent.append(copy)

    for chunk in range(chunks):
        base = chunk * chunk_rows
        for kind in range(3):
            own_copies[chunk * 3 + kind].wait()
        for offset in range(1, groups):
            source = lax.rem(me + groups - offset, groups)
            for kind, pair in enumerate(in_pairs(me, source, chunk)):
                remote(
                    pair, in_send.at[chunk, kind, offset], in_recv.at[chunk, kind, offset], source
                ).wait_recv()

        @pl.loop(0, chunk_rows // group_rows)
        def _(step):
            inner = pl.ds(pl.multiple_of(step * group_rows, group_rows), group_rows)
            picked = pl.ds(pl.multiple_of(base + step * group_rows, group_rows), group_rows)
            primed = []
            for stream in range(3):
                wide = tokens_of(stream, picked).astype(jnp.float32)
                running = column(stream * taps, picked) * wide
                for offset in range(1, taps):
                    running = running + column(stream * taps + offset, picked) * delayed(
                        wide, offset
                    )
                primed.append(running)
                primed_buf[stream, inner, :] = running
            stacked[0, inner, :] = (primed[1] * primed[2]).astype(jnp.bfloat16)
            cot_wide = tokens_of(3, picked).astype(jnp.float32)
            stacked[1, inner, :] = (cot_wide * primed[0]).astype(jnp.bfloat16)
            stacked[2, inner, :] = tokens_of(4, picked)

        tile = 512

        @pl.loop(0, 2 * length // tile)
        def _(step):
            columns = pl.ds(pl.multiple_of(step * tile, tile), tile)
            left = stacked[...].reshape(3 * chunk_rows, length)
            total = jnp.dot(left, table[0, :, columns], preferred_element_type=jnp.float32)
            total += jnp.dot(left, table[1, :, columns], preferred_element_type=jnp.float32)
            freq[:, :, columns] = total.reshape(3, chunk_rows, tile)

        @pl.loop(0, chunk_rows // group_rows)
        def _(step):
            inner = pl.ds(pl.multiple_of(step * group_rows, group_rows), group_rows)
            first = lax.broadcasted_iota(jnp.int32, (group_rows, length), 1) == 0
            weight = jnp.where(first, 0.5 * scale, scale)
            mix_c, mix_s = freq[0, inner, :length], freq[0, inner, length:]
            grad_c, grad_s = freq[1, inner, :length], freq[1, inner, length:]
            kern_c, kern_s = freq[2, inner, :length], freq[2, inner, length:]

            def put(slot, left_c, left_s, right_c, right_s, sign):
                both = left_s * right_s
                even = left_c * right_c + sign * jnp.where(first, 0.0, both)
                odd = jnp.where(first, both, left_s * right_c - sign * (left_c * right_s))
                for half, part in enumerate((even, odd)):
                    value = part * weight
                    high = value.astype(jnp.bfloat16)
                    low = (value - high.astype(jnp.float32)).astype(jnp.bfloat16)
                    back_both[slot, inner, half * length : (half + 1) * length] = high
                    back_both[3 + slot, inner, half * length : (half + 1) * length] = low

            put(0, mix_c, mix_s, kern_c, kern_s, -1.0)
            put(1, grad_c, grad_s, kern_c, kern_s, 1.0)
            put(2, grad_c, grad_s, mix_c, mix_s, 1.0)

        @pl.loop(0, length // tile)
        def _(step):
            picked = pl.ds(pl.multiple_of(step * tile, tile), tile)
            both = back_both[...].reshape(6 * chunk_rows, 2 * length)
            high = both[: 3 * chunk_rows]
            turned = (((1,), (1,)), ((), ()))
            pair = lax.dot_general(
                both, table[0, picked, :], turned, preferred_element_type=jnp.float32
            )
            total = pair[: 3 * chunk_rows] + pair[3 * chunk_rows :]
            total += lax.dot_general(
                high, table[1, picked, :], turned, preferred_element_type=jnp.float32
            )
            back_time[:, :, picked] = total.reshape(3, chunk_rows, tile)

        finish(4, pl.ds(base, chunk_rows), back_time[2])
        send_kinds(chunk, (2,))
        whole = pl.ds(base, chunk_rows)
        with_gain = back_time[0] + column(3 * taps, whole) * stacked[0].astype(jnp.float32)
        back_time[0] = with_gain.astype(jnp.bfloat16).astype(jnp.float32)
        finish(0, whole, primed_buf[0] * back_time[0])
        send_kinds(chunk, (0,))

        @pl.loop(0, chunk_rows // group_rows)
        def _(step):
            inner = pl.ds(pl.multiple_of(step * group_rows, group_rows), group_rows)
            picked = pl.ds(pl.multiple_of(base + step * group_rows, group_rows), group_rows)
            mixed = stacked[0, inner, :].astype(jnp.float32)
            gated = stacked[1, inner, :].astype(jnp.float32)
            gain = column(3 * taps, picked)
            long_wide = back_time[0, inner, :]
            mixed_back = (
                (back_time[1, inner, :] + gain * gated).astype(jnp.bfloat16).astype(jnp.float32)
            )
            cot_wide = tokens_of(3, picked).astype(jnp.float32)
            primed_grad = [
                cot_wide * long_wide,
                mixed_back * primed_buf[2, inner, :],
                mixed_back * primed_buf[1, inner, :],
            ]
            lane = lax.broadcasted_iota(jnp.int32, (group_rows, sums.shape[1]), 1)
            line = jnp.zeros((group_rows, sums.shape[1]), jnp.float32)
            for stream in range(3):
                moving = primed_grad[stream]
                wide = tokens_of(stream, picked).astype(jnp.float32)
                running = column(stream * taps, picked) * moving
                for offset in range(taps):
                    if offset:
                        running = running + column(stream * taps + offset, picked) * advanced(
                            moving, offset
                        )
                    total = jnp.sum(moving * delayed(wide, offset), axis=1, keepdims=True)
                    line = jnp.where(lane == stream * taps + offset, total, line)
                finish(1 + stream, picked, running)
            total = jnp.sum(gated * mixed, axis=1, keepdims=True)
            sums[picked, :] = jnp.where(lane == 3 * taps, total, line)

        send_kinds(chunk, (1,))
        for kind, pair in enumerate(out_pairs(me, me, chunk)):
            copy = pltpu.make_async_copy(pair[0], pair[1], own_out.at[chunk, kind])
            copy.start()
            own_copies.append(copy)

    turned_sums = sums[...].T
    for stream in range(3):
        taps_out[stream] = turned_sums[stream * taps : (stream + 1) * taps, :]
    skip_out[...] = turned_sums[3 * taps : 3 * taps + 1, :]

    def small_pairs(owner):
        return [
            (taps_out, taps_hbm.at[:, :, at(owner, rows)]),
            (skip_out, skip_hbm.at[:, at(owner, rows)]),
        ]

    for kind, pair in enumerate(small_pairs(me)):
        copy = pltpu.make_async_copy(pair[0], pair[1], small_own.at[kind])
        copy.start()
        own_copies.append(copy)
        for offset in range(1, groups):
            peer = lax.rem(me + offset, groups)
            copy = remote(pair, small_send.at[kind, offset], small_recv.at[kind, offset], peer)
            copy.start()
            sent.append(copy)
    for copy in sent:
        copy.wait_send()
    for copy in own_copies[3 * chunks :]:
        copy.wait()
    for offset in range(1, groups):
        source = lax.rem(me + groups - offset, groups)
        for chunk in range(chunks):
            for kind, pair in enumerate(out_pairs(me, source, chunk)):
                remote(
                    pair, out_send.at[chunk, kind, offset], out_recv.at[chunk, kind, offset], source
                ).wait_recv()
        for kind, pair in enumerate(small_pairs(source)):
            remote(
                pair, small_send.at[kind, offset], small_recv.at[kind, offset], source
            ).wait_recv()


def settle_kernel(*refs):
    count = len(refs) // 2
    finished = refs[2 * count]
    copies = []
    for index in range(count):
        copy = pltpu.make_async_copy(refs[index], refs[count + index], finished.at[index])
        copy.start()
        copies.append(copy)
    for copy in copies:
        copy.wait()


def settle(values):
    return pl.pallas_call(
        settle_kernel,
        out_shape=tuple(jax.ShapeDtypeStruct(value.shape, value.dtype) for value in values),
        in_specs=[pl.BlockSpec(memory_space=pltpu.VMEM)] * len(values),
        out_specs=(pl.BlockSpec(memory_space=pltpu.HBM),) * len(values),
        scratch_shapes=[pltpu.SemaphoreType.DMA((len(values),))],
    )(*values)


def fused(features, cotangent, long_filter, short_filters, skip_gain, groups, chunks):
    channels, span = cotangent.shape
    rows = channels // groups
    length = span * groups
    taps = short_filters.shape[2]
    chunk_rows = rows // chunks
    hbm = pl.BlockSpec(memory_space=pltpu.HBM)
    dma = pltpu.SemaphoreType.DMA
    narrow = jnp.bfloat16
    outputs = pl.pallas_call(
        functools.partial(fused_kernel, (groups, rows, span, length, taps, chunks)),
        out_shape=(
            jax.ShapeDtypeStruct((channels, span), narrow),
            jax.ShapeDtypeStruct((3, channels, span), narrow),
            jax.ShapeDtypeStruct((channels, span), narrow),
            jax.ShapeDtypeStruct((3, taps, channels), jnp.float32),
            jax.ShapeDtypeStruct((1, channels), jnp.float32),
        ),
        in_specs=[hbm] * 6,
        out_specs=(pl.BlockSpec(memory_space=pltpu.VMEM),) * 5,
        scratch_shapes=[
            pltpu.VMEM((2, length, 2 * length), narrow),
            pltpu.VMEM((3, taps, rows), jnp.float32),
            pltpu.VMEM((1, channels), jnp.float32),
            pltpu.VMEM((rows, rows), jnp.float32),
            pltpu.VMEM((rows, rows), jnp.float32),
            pltpu.VMEM((groups, 5, rows, span), narrow),
            pltpu.VMEM((3, chunk_rows, length), narrow),
            pltpu.VMEM((3, chunk_rows, length), jnp.float32),
            pltpu.VMEM((3, chunk_rows, 2 * length), jnp.float32),
            pltpu.VMEM((6, chunk_rows, 2 * length), narrow),
            pltpu.VMEM((3, chunk_rows, length), jnp.float32),
            pltpu.VMEM((groups, 5, rows, span), narrow),
            pltpu.VMEM((rows, rows), jnp.float32),
            pltpu.VMEM((3, taps, rows), jnp.float32),
            pltpu.VMEM((1, rows), jnp.float32),
            dma((3,)),
            dma((chunks, 3)),
            dma((chunks, 3)),
            dma((chunks, 3, groups)),
            dma((chunks, 3, groups)),
            dma((chunks, 3, groups)),
            dma((chunks, 3, groups)),
            dma((2,)),
            dma((2, groups)),
            dma((2, groups)),
        ],
        compiler_params=pltpu.CompilerParams(
            collective_id=0, has_side_effects=True
        ),
    )(
        features,
        cotangent,
        long_filter,
        jnp.swapaxes(short_filters, 1, 2),
        skip_gain[None],
        packed_tables(length),
    )
    gated_out, feature_grad, long_grad, taps_grad, gain_grad = settle(outputs)
    return gated_out, feature_grad, long_grad, jnp.swapaxes(taps_grad, 1, 2), gain_grad[0]


def dense_fits(features, short_filters, groups):
    channels, span = features.shape[1:]
    rows, length = channels // groups, span * groups
    return (
        channels % groups == 0
        and rows % 128 == 0
        and span % 128 == 0
        and length % 512 == 0
        and length <= 1024
        and rows <= 256
        and 3 * short_filters.shape[2] < 16
    )


def shards(features, cotangent, long_filter, short_filters, skip_gain):
    groups = lax.axis_size("seq")
    if dense_fits(features, short_filters, groups):
        return fused(
            features, cotangent, long_filter, short_filters, skip_gain, groups, chunk_count
        )
    seq_index = lax.axis_index("seq")
    channels = features.shape[1]
    per_group = channels // groups
    margin = short_filters.shape[2] - 1
    local_gain = lax.dynamic_slice_in_dim(skip_gain, seq_index * per_group, per_group, 0)
    stacked = jnp.concatenate([features, cotangent[None], long_filter[None]], 0)
    columns = lax.all_to_all(stacked, "seq", split_axis=1, concat_axis=2, tiled=True)
    weights = lax.dynamic_slice_in_dim(short_filters, seq_index * per_group, per_group, 1)
    length = columns.shape[2]
    history = jnp.pad(columns[:3].astype(jnp.float32), ((0, 0), (0, 0), (margin, 0)))
    primed = featurize(history, weights, margin, length)
    mixed_term = (primed[1] * primed[2]).astype(jnp.bfloat16)
    cot_wide = columns[3].astype(jnp.float32)
    gated_grad = (cot_wide * primed[0]).astype(jnp.bfloat16)
    long_out, mixed_grad, kernel_grad = spectral(mixed_term, gated_grad, columns[4], local_gain)
    long_wide = long_out.astype(jnp.float32)
    mixed_back = mixed_grad.astype(jnp.float32)
    gated_out = (primed[0] * long_wide).astype(jnp.bfloat16)
    primed_grad = jnp.stack([cot_wide * long_wide, mixed_back * primed[2], mixed_back * primed[1]])
    padded_grad = jnp.pad(primed_grad, ((0, 0), (0, 0), (0, margin)))
    feature_grad = unfeaturize(padded_grad, weights, length).astype(jnp.bfloat16)
    taps_grad = tap_grads(primed_grad, history, margin, length)
    gain_grad = jnp.sum(gated_grad.astype(jnp.float32) * mixed_term.astype(jnp.float32), axis=-1)
    results = jnp.concatenate([gated_out[None], feature_grad, kernel_grad[None]], 0)
    row_blocks = lax.all_to_all(results, "seq", split_axis=2, concat_axis=1, tiled=True)
    short_grad, skip_grad = (
        lax.all_gather(taps_grad, "seq", axis=1, tiled=True),
        lax.all_gather(gain_grad, "seq", axis=0, tiled=True),
    )
    return (row_blocks[0], row_blocks[1:4], row_blocks[4], short_grad, skip_grad)


def solution(mesh):
    placed = (
        P(None, "chan", "seq"),
        P("chan", "seq"),
        P("chan", "seq"),
        P(None, "chan", None),
        P("chan"),
    )
    return jax.shard_map(
        shards,
        mesh=mesh,
        in_specs=placed,
        out_specs=(
            P("chan", "seq"),
            P(None, "chan", "seq"),
            P("chan", "seq"),
            P(None, "chan", None),
            P("chan"),
        ),
        check_vma=False,
    )
```
